512 devices in a mesh: seq: 64 (over y_hi, z, core), mp: 8 (over y_lo, x).
Axes of the slice: x: 4, y: 8 (y_hi: 4, y_lo: 2; y = y_hi * 2 + y_lo), z: 8, core: 2. Of those that a mesh axis runs over, the one named last changes fastest.
Arguments:
- queries: bfloat16 [16384, 8, 64], P('seq', 'mp'), may hold values from -6 to 6
- key_value: bfloat16 [16384, 8, 128], P('seq', 'mp'), may hold values from -6 to 6
- tile_fill: int32 [128], P('seq'), may hold values from 0 to 128, as said below
- out_weight: bfloat16 [8, 64, 768], P('mp'), may hold values from -0.75 to 0.75
- grad_output: bfloat16 [16384, 768], P('seq'), may hold values from -6 to 6
Outputs:
- attention_out: bfloat16 [16384, 768], P('seq')
- query_grad: float32 [16384, 8, 64], P('seq', 'mp')
- key_value_grad: float32 [16384, 8, 128], P('seq', 'mp')
- out_weight_grad: float32 [8, 64, 768], P('mp')
The draws below stay inside these ranges and needn't reach their ends.
Inputs may be any that keep to these rules, and one draw needn't show every extreme that they name: `tile_fill`: tile 0 is full, and the first tile of every block of 256 slots holds at least one active voxel.
All inputs are finite; a program needn't handle non-finite values.
Results may differ from the reference program's by a relative error of at most 0.03.
Values may be sent and summed in bfloat16 or wider, within the bound.
A program may use at most 64 MiB of HBM per device.

```python
import jax
import jax.numpy as jnp
from jax import lax

D = 768
HEADS = 8
DH = 64
TILE = 128
TOK_DEV = 256
TOKENS = 16384


def rough_field(key, shape):
    return jnp.clip(jax.random.normal(key, shape, jnp.float32) * 1.58, -6.0, 6.0)


def draw_queries(key, part):
    values = rough_field(jax.random.fold_in(key, 1), (TOKENS, HEADS, DH))
    return values.astype(jnp.bfloat16)


def draw_key_value(key, part):
    values = rough_field(jax.random.fold_in(key, 2), (TOKENS, HEADS, 2 * DH))
    return values.astype(jnp.bfloat16)


def draw_tile_fill(key, part):
    tiles = TOKENS // TILE
    per_device = TOK_DEV // TILE
    devices = TOKENS // TOK_DEV
    level_key, fill_key, empty_key = jax.random.split(jax.random.fold_in(key, 11), 3)
    levels = jax.random.randint(level_key, (devices,), 1, 5)
    tile_index = jnp.arange(tiles, dtype=jnp.int32)
    tile_level = levels[tile_index // per_device]
    uniform_fill = jax.random.randint(fill_key, (tiles,), 0, TILE)
    empty_draw = jax.random.randint(empty_key, (tiles,), 0, 8)
    filled = TILE - uniform_fill * (5 - tile_level) // 8
    first_tile = tile_index % per_device == 0
    empty_tile = jnp.logical_and(empty_draw >= tile_level + 5, jnp.logical_not(first_tile))
    filled = jnp.where(empty_tile, 0, filled)
    filled = filled.at[0].set(TILE)
    return filled.astype(jnp.int32)


def steps_of(stream_key, shape, cuts, least, largest):
    factor_of, own = 1.0, jax.random.fold_in(stream_key, 6)
    for axis_at, shards_of in cuts:
        draws = jnp.exp(jax.random.uniform(jax.random.fold_in(own, axis_at), (shards_of,), jnp.float32, least / len(cuts), largest / len(cuts)))
        factor_of = factor_of * jnp.repeat(draws, shape[axis_at] // shards_of).reshape([-1 if axis == axis_at else 1 for axis in range(len(shape))])
    return factor_of


def gaussian(stream_key, extent, deviation, reach, cuts=(), kind=jnp.bfloat16):
    level = steps_of(stream_key, extent, cuts, -0.22, 0.18) if cuts else 1.0
    result = jax.random.normal(stream_key, extent, jnp.float32) * deviation * level
    return jnp.minimum(jnp.maximum(result, -reach), reach).astype(kind)


def setup_inputs(seed: int = 0) -> dict:
    splits = jax.random.split(jax.random.key(seed), 6)
    return {
        "queries": draw_queries(jax.random.fold_in(splits[5], 71), 0),
        "key_value": draw_key_value(jax.random.fold_in(splits[5], 71), 0),
        "tile_fill": draw_tile_fill(jax.random.fold_in(splits[5], 71), 0),
        "out_weight": gaussian(splits[3], (HEADS, DH, D), DH ** -0.5, 0.75, ((0, 8),)),
        "grad_output": gaussian(splits[4], (TOKENS, D), 1.0, 6.0, ((0, 64),)),
    }


def live_slots(tile_fill):
    within = lax.iota(jnp.int32, TILE)
    return (within[None, :] < tile_fill[:, None]).reshape(-1)


def reference(queries, key_value, tile_fill, out_weight, grad_output):
    live_mask = live_slots(tile_fill)
    score_scale = DH ** -0.5
    number = TOKENS // TOK_DEV
    q_heads = jnp.transpose(queries, (1, 0, 2))
    k_heads = jnp.transpose(key_value[:, :, :DH], (1, 0, 2))
    v_heads = jnp.transpose(key_value[:, :, DH:], (1, 0, 2))

    def forward_head(operands):
        q_one, k_one, v_one = operands

        def forward_block(q_block):
            scores = jnp.dot(q_block, k_one.T, preferred_element_type=jnp.float32) * score_scale
            masked = jnp.where(live_mask[None, :], scores, -jnp.inf)
            row_peak = jnp.max(masked, axis=1)
            log_total = row_peak + jnp.log(jnp.sum(jnp.exp(masked - row_peak[:, None]), axis=1))
            weights = jnp.where(live_mask[None, :], jnp.exp(scores - log_total[:, None]), 0.0).astype(jnp.bfloat16)
            attended = jnp.dot(weights, v_one, preferred_element_type=jnp.float32).astype(jnp.bfloat16)
            return attended, log_total

        attended, log_total = lax.map(forward_block, q_one.reshape(number, TOK_DEV, DH))
        return attended.reshape(TOKENS, DH), log_total.reshape(TOKENS)

    attended, log_total = lax.map(forward_head, (q_heads, k_heads, v_heads))
    live_float = live_mask.astype(jnp.float32)
    projected = jnp.einsum("hqd,hde->qe", attended.astype(jnp.float32), out_weight.astype(jnp.float32))
    attention_out = (projected * live_float[:, None]).astype(jnp.bfloat16)
    grad_mixed = grad_output * live_mask[:, None].astype(jnp.bfloat16)
    grad_attn = jnp.einsum("qe,hde->hqd", grad_mixed.astype(jnp.float32), out_weight.astype(jnp.float32)).astype(jnp.bfloat16)
    out_weight_grad = jnp.einsum("hqd,qe->hde", attended.astype(jnp.float32), grad_mixed.astype(jnp.float32))
    inner_sum = jnp.sum(grad_attn.astype(jnp.float32) * attended.astype(jnp.float32), axis=2)

    def backward_head(operands):
        q_one, k_one, v_one, log_one, grad_one, inner_one = operands

        def backward_block(carried, pieces):
            grad_keys, grad_values = carried
            q_block, log_block, grad_block, inner_block = pieces
            scores = jnp.dot(q_block, k_one.T, preferred_element_type=jnp.float32) * score_scale
            prob_rows = jnp.where(live_mask[None, :], jnp.exp(scores - log_block[:, None]), 0.0)
            grad_probs = jnp.dot(grad_block, v_one.T, preferred_element_type=jnp.float32)
            grad_scores = (prob_rows * (grad_probs - inner_block[:, None])).astype(jnp.bfloat16)
            grad_query = jnp.dot(grad_scores, k_one, preferred_element_type=jnp.float32) * score_scale
            grad_keys = grad_keys + jnp.dot(grad_scores.T, q_block, preferred_element_type=jnp.float32) * score_scale
            grad_values = grad_values + jnp.dot(prob_rows.astype(jnp.bfloat16).T, grad_block, preferred_element_type=jnp.float32)
            return (grad_keys, grad_values), grad_query

        start_zero = jnp.zeros((TOKENS, DH), jnp.float32)
        blocked = (q_one.reshape(number, TOK_DEV, DH), log_one.reshape(number, TOK_DEV),
                   grad_one.reshape(number, TOK_DEV, DH), inner_one.reshape(number, TOK_DEV))
        (grad_keys, grad_values), grad_query = lax.scan(backward_block, (start_zero, start_zero), blocked)
        return grad_query.reshape(TOKENS, DH), grad_keys, grad_values

    grad_query, grad_keys, grad_values = lax.map(backward_head, (q_heads, k_heads, v_heads, log_total, grad_attn, inner_sum))
    query_grad = jnp.transpose(grad_query, (1, 0, 2))
    key_value_grad = jnp.concatenate([jnp.transpose(grad_keys, (1, 0, 2)), jnp.transpose(grad_values, (1, 0, 2))], axis=2)
    return attention_out, query_grad, key_value_grad, out_weight_grad
```

```python
import functools

import jax
import jax.numpy as jnp
from jax import lax
from jax.experimental import pallas as pl
from jax.experimental.pallas import tpu as pltpu
from jax.sharding import PartitionSpec as P

MESH = pl.DeviceIdType.MESH
BF = jnp.bfloat16
F32 = jnp.float32
TILE = 128
DH = 64
CORES = 2


def nn(a, b):
    return jnp.dot(a, b, preferred_element_type=F32)


def nt(a, b):
    return lax.dot_general(a, b, (((1,), (1,)), ((), ())), preferred_element_type=F32)


def place(offset, size):
    o = offset % size
    if o > size // 2:
        o -= size
    return 2 * o - 1 if o > 0 else -2 * o


def offset_of(rank):
    half = (rank + 1) // 2
    return half if rank % 2 == 1 else -half


def kernel(
    NY, NZ, NMP,
    fill_ref, qT_ref, kv_ref, w_ref, g_ref,
    out_ref, dq_ref, dkv_ref, wg_ref,
    kvb, kvT, qd, qS, dO, p, mh, m, oacc, ab,
    sA, sB, uoA, uoB, dsA, dsB,
    stl, str_, Lg, Dg, osend, orecv, dkacc, dsend, drecv, dqacc, dqsend, dqrecv,
    gmb, wall, attall, wg1s, wg1r, wg2, wg3,
    kv_s, kv_r, q_s, q_r, rl_s, st_s, st_r, o_s, o_r, dk_s, dk_r, dq_s, dq_r,
    w_s, w_r, at_s, at_r, g1_s, g1_r, g2_s, g2_r, g3_s, g3_r,
):
    T = kv_ref.shape[0]
    D = w_ref.shape[1]
    NB, NQ = NZ, NY * CORES
    U = NQ // 2
    RW = DH // NQ

    seq = lax.axis_index("seq")
    mp = lax.axis_index("mp")
    core = seq % CORES
    z = (seq // CORES) % NZ
    y = seq // (CORES * NZ)

    def zdev(o):
        return ((y * NZ + (z + o + NZ) % NZ) * CORES + core, mp)

    def qoff(i):
        return offset_of(i // 2) % NY, i % 2

    def qdev(i):
        dy, dc = qoff(i)
        return ((((y + dy) % NY) * NZ + z) * CORES + (core + dc) % 2, mp)

    def qabs(i):
        dy, dc = qoff(i)
        return ((y + dy) % NY) * CORES + (core + dc) % 2

    def qback(i):
        dy, dc = qoff(i)
        return 2 * place(-dy, NY) + dc

    def mdev(r):
        return (seq, (mp + r) % NMP)

    partner = qdev(1)

    def rcopy(src, dst, ssem, rsem, dev):
        return pltpu.make_async_remote_copy(
            src_ref=src, dst_ref=dst, send_sem=ssem, recv_sem=rsem, device_id=dev, device_id_type=MESH
        )

    barrier = pltpu.get_barrier_semaphore()
    for j in range(1, NB):
        pl.semaphore_signal(barrier, inc=1, device_id=zdev(offset_of(j)), device_id_type=MESH)
    for i in range(1, NQ):
        pl.semaphore_signal(barrier, inc=1, device_id=qdev(i), device_id_type=MESH)
    for r in range(1, NMP):
        pl.semaphore_signal(barrier, inc=1, device_id=mdev(r), device_id_type=MESH)

    rows = lax.broadcasted_iota(jnp.int32, (T, 1), 0)
    fills = [fill_ref[t] for t in range(T // TILE)]
    live_col = jnp.zeros((T, 1), F32)
    for t in range(T // TILE):
        inside = (rows >= t * TILE) & (rows < t * TILE + fills[t])
        live_col = jnp.where(inside, 1.0, live_col)
    lanes = lax.broadcasted_iota(jnp.int32, (1, T), 1)
    live_row = jnp.zeros((1, T), F32)
    for t in range(T // TILE):
        inside = (lanes >= t * TILE) & (lanes < t * TILE + fills[t])
        live_row = jnp.where(inside, 1.0, live_row)
    kv = kv_ref[...].astype(F32)
    is_key = lax.broadcasted_iota(jnp.int32, (1, 2 * DH), 1) < DH
    stand_in = jnp.where(is_key, kv[0:1, :], 0.0)
    kvb[0, 0:T, :] = jnp.where(live_col > 0.0, kv, stand_in).astype(BF)
    tail_rows = lax.broadcasted_iota(jnp.int32, (16, 1), 0)
    tail = jnp.zeros((16, TILE), F32)
    for t in range(T // TILE):
        tail = jnp.where(tail_rows == t, live_row[:, t * TILE : (t + 1) * TILE], tail)
    kvb[0, T : T + 16, :] = tail.astype(BF)

    pl.semaphore_wait(barrier, (NB - 1) + (NQ - 1) + (NMP - 1))

    kv_copies = []
    for j in range(1, NB):
        o = offset_of(j)
        back = place(-o, NZ)
        c = rcopy(kvb.at[0], kvb.at[back], kv_s.at[j], kv_r.at[back], zdev(o))
        c.start()
        kv_copies.append(c)

    gmb[...] = (g_ref[...].astype(F32) * live_col).astype(BF)
    qd[0, 0:DH, :] = (qT_ref[...].astype(F32) * (DH**-0.5)).astype(BF)
    qd[0, DH : 2 * DH, :] = nt(w_ref[...], gmb[...]).astype(BF)

    q_copies = []
    c = rcopy(qd.at[0], qd.at[1], q_s.at[1], q_r.at[1], partner)
    c.start()
    q_copies.append(c)
    for k in range(1, NY):
        i = 2 * k
        back = qback(i)
        c = rcopy(qd.at[0], qd.at[back], q_s.at[i], q_r.at[back], qdev(i))
        c.start()
        q_copies.append(c)

    def prepare_keys(j):
        live16 = kvb[j, T : T + 16, :].astype(F32)
        row = jnp.concatenate([live16[t : t + 1, :] for t in range(T // TILE)], axis=1)
        kvT[j, 0 : 2 * DH, :] = (kvb[j, 0:T, :].astype(F32).T * row).astype(BF)
        kvT[j, 2 * DH : 2 * DH + 16, :] = jnp.broadcast_to(row, (16, T)).astype(BF)

    def prepare_queries(i):
        qS[i, 0:DH, :] = qd[i, 0:DH, :]
        dO[i] = qd[i, DH : 2 * DH, :]

    for i in range(NQ):
        m[i] = jnp.full((8, T), -1e30, F32)
        oacc[i] = jnp.zeros((DH + 16, T), F32)
        dqacc[i] = jnp.zeros((DH, T), F32)
        qS[i, DH : 2 * DH, :] = jnp.zeros((DH, T), BF)
    for t in range(U):
        uoA[t, 0:DH, :] = jnp.zeros((DH, T), BF)
        uoB[t, 0:DH, :] = jnp.zeros((DH, T), BF)
    prepare_keys(0)
    prepare_queries(0)

    for k in range(1, NY):
        i = 2 * k
        rcopy(qd.at[0], qd.at[i], q_s.at[i], q_r.at[i], partner).wait_recv()
        c = rcopy(qd.at[i], qd.at[i + 1], rl_s.at[i], q_r.at[i + 1], partner)
        c.start()
        q_copies.append(c)
        prepare_queries(i)

    wall[mp] = w_ref[...]
    w_copies = []
    for r in range(1, NMP):
        c = rcopy(wall.at[mp], wall.at[mp], w_s.at[r], w_r.at[r], mdev(r))
        c.start()
        w_copies.append(c)

    for k in range(NY):
        i = 2 * k + 1
        rcopy(qd.at[0], qd.at[i], q_s.at[i], q_r.at[i], partner).wait_recv()
        prepare_queries(i)

    def S(j, half, buf):
        for t in range(U):
            buf[t] = nn(kvb[j, 0:T, :], qS[half * U + t])

    def E(j, half, buf):
        for t in range(U):
            i = half * U + t
            m_old = m[i, 0:1, :]
            m_new = jnp.maximum(m_old, jnp.max(buf[t], axis=0, keepdims=True))
            mh[j, i, 0:1, :] = m_new
            m[i, 0:1, :] = m_new
            ab[half, t, 0:1, :] = jnp.exp(m_old - m_new)
            p[j, i] = jnp.exp(buf[t] - m_new).astype(BF)

    def O(j, half):
        for t in range(U):
            i = half * U + t
            oacc[i] = oacc[i] * ab[half, t, 0:1, :] + nn(kvT[j, DH : 2 * DH + 16, :], p[j, i])

    S(0, 0, sA)
    E(0, 0, sA)
    S(0, 1, sB)

    @pl.loop(1, NB)
    def _(j):
        rcopy(kvb.at[0], kvb.at[j], kv_s.at[j], kv_r.at[j], partner).wait_recv()
        prepare_keys(j)
        S(j, 0, sA)
        E(j - 1, 1, sB)
        O(j - 1, 0)
        S(j, 1, sB)
        E(j, 0, sA)
        O(j - 1, 1)

    E(NB - 1, 1, sB)
    O(NB - 1, 0)
    O(NB - 1, 1)

    for i in range(NQ):
        acc = oacc[i]
        total = acc[DH : DH + 1, :]
        o = acc[0:DH, :] * (1.0 / total)
        osend[i] = o.astype(BF)
        row = qabs(i)
        stl[pl.ds(row, 1), :] = m[i, 0:1, :] + jnp.log(total)
        stl[pl.ds(NQ + row, 1), :] = jnp.sum(o * dO[i].astype(F32), axis=0, keepdims=True)

    st_copies = []
    for i in range(1, NQ):
        back = qback(i)
        c = rcopy(stl, str_.at[back], st_s.at[i], st_r.at[back], qdev(i))
        c.start()
        st_copies.append(c)
    o_copies = []
    for i in range(1, NQ):
        back = qback(i)
        c = rcopy(osend.at[i], orecv.at[back], o_s.at[i], o_r.at[back], qdev(i))
        c.start()
        o_copies.append(c)
    str_[0] = stl[...]
    for i in range(1, NQ):
        rcopy(stl, str_.at[i], st_s.at[i], st_r.at[i], partner).wait_recv()
    big = str_[0, 0:NQ, :]
    for s in range(1, NQ):
        big = jnp.maximum(big, str_[s, 0:NQ, :])
    wsum = jnp.zeros((NQ, T), F32)
    dsum = jnp.zeros((NQ, T), F32)
    for s in range(NQ):
        wt = jnp.exp(str_[s, 0:NQ, :] - big)
        wsum = wsum + wt
        dsum = dsum + wt * str_[s, NQ : 2 * NQ, :]
    stl2 = big + jnp.log(wsum)
    Lg[NQ, 0:NQ, :] = stl2
    Dg[NQ, 0:NQ, :] = dsum / wsum
    for i in range(NQ):
        Lg[i, 0:1, :] = Lg[NQ, pl.ds(qabs(i), 1), :]
        Dg[i, 0:1, :] = Dg[NQ, pl.ds(qabs(i), 1), :]

    def Ust(j, half, buf, uo):
        for t in range(U):
            i = half * U + t
            c = jnp.exp(mh[j, i, 0:1, :] - Lg[i, 0:1, :])
            cdo = (dO[i].astype(F32) * c).astype(BF)
            uo[t, DH : 2 * DH, :] = cdo
            rhs = jnp.concatenate([jnp.zeros((DH, T), BF), cdo], axis=0)
            buf[t] = nn(kvb[j, 0:T, :], rhs) - c * Dg[i, 0:1, :]

    def Dst(j, half, buf, ds):
        for t in range(U):
            ds[t] = (p[j, half * U + t].astype(F32) * buf[t]).astype(BF)

    def Mst(j, half, ds, uo):
        acc = None
        for t in range(U):
            i = half * U + t
            dqacc[i] += nn(kvT[j, 0:DH, :], ds[t])
            r = nt(ds[t], qS[i]) + nt(p[j, i], uo[t])
            acc = r if acc is None else acc + r
        if half == 0:
            dkacc[...] = acc
        else:
            dkacc[...] += acc

    def dk_copy(j):
        half = (j + 1) // 2
        odd = j % 2
        o = (2 * odd - 1) * half
        back = jnp.where(half * 2 == NZ, j, j + 2 * odd - 1)
        return rcopy(dsend.at[j], drecv.at[back], dk_s.at[j], dk_r.at[back], zdev(o))

    def turn(n):
        done = n + 1
        Mst(done, 0, dsA, uoA)
        Dst(done, 1, sB, dsB)
        Ust(n, 0, sA, uoA)
        Mst(done, 1, dsB, uoB)
        dsend[done] = dkacc[...].astype(BF)
        dk_copy(done).start()
        Dst(n, 0, sA, dsA)
        Ust(n, 1, sB, uoB)

    Ust(NB - 1, 0, sA, uoA)
    Dst(NB - 1, 0, sA, dsA)
    Ust(NB - 1, 1, sB, uoB)

    first = (NB - 1) // 2

    @pl.loop(0, first)
    def _(t):
        turn(NB - 2 - t)

    att = jnp.zeros((DH, T), F32)
    for i in range(1, NQ):
        rcopy(osend.at[i], orecv.at[i], o_s.at[i], o_r.at[i], partner).wait_recv()
    orecv[0] = osend[0]
    for s in range(NQ):
        wt = jnp.exp(str_[s, pl.ds(qabs(0), 1), :] - Lg[0, 0:1, :])
        att = att + wt * orecv[s].astype(F32)
    attall[mp] = (att * live_row).astype(BF)
    at_copies = []
    for r in range(1, NMP):
        c = rcopy(attall.at[mp], attall.at[mp], at_s.at[r], at_r.at[r], mdev(r))
        c.start()
        at_copies.append(c)
    wgp = nn(att.astype(BF), gmb[...])
    for s in range(NQ):
        wg1s[s] = wgp[s * RW : (s + 1) * RW, :].astype(BF)
    g1_copies = []
    for i in range(1, NQ):
        back = qback(i)
        c = rcopy(wg1s.at[qabs(i)], wg1r.at[back], g1_s.at[i], g1_r.at[back], qdev(i))
        c.start()
        g1_copies.append(c)

    @pl.loop(first, NB - 1)
    def _(t):
        turn(NB - 2 - t)

    Mst(0, 0, dsA, uoA)
    Dst(0, 1, sB, dsB)
    Mst(0, 1, dsB, uoB)

    dq_copies = []
    for i in range(1, NQ):
        dqsend[i] = (dqacc[i] * (DH**-0.5)).astype(BF)
        back = qback(i)
        c = rcopy(dqsend.at[i], dqrecv.at[back], dq_s.at[i], dq_r.at[back], qdev(i))
        c.start()
        dq_copies.append(c)

    wg1r[0] = wg1s[qabs(0)]
    for i in range(1, NQ):
        rcopy(wg1s.at[0], wg1r.at[i], g1_s.at[i], g1_r.at[i], partner).wait_recv()
    part = wg1r[0].astype(F32)
    for i in range(1, NQ):
        part = part + wg1r[i].astype(F32)
    wg2[z] = part.astype(BF)
    g2_copies = []
    for r in range(1, NZ):
        c = rcopy(wg2.at[z], wg2.at[z], g2_s.at[r], g2_r.at[r], zdev(r))
        c.start()
        g2_copies.append(c)

    for r in range(1, NMP):
        rcopy(wall.at[0], wall.at[0], w_s.at[r], w_r.at[r], partner).wait_recv()
        rcopy(attall.at[0], attall.at[0], at_s.at[r], at_r.at[r], partner).wait_recv()
    att_rows = attall[...].reshape(NMP * DH, T).astype(F32).T.astype(BF)
    out_ref[...] = nn(att_rows, wall[...].reshape(NMP * DH, D)).astype(BF)

    for r in range(1, NZ):
        rcopy(wg2.at[0], wg2.at[0], g2_s.at[r], g2_r.at[r], partner).wait_recv()
    part = wg2[0].astype(F32)
    for k in range(1, NZ):
        part = part + wg2[k].astype(F32)
    own = qabs(0)
    wg3[own] = part.astype(BF)
    g3_copies = []
    for i in range(1, NQ):
        back = qback(i)
        c = rcopy(wg3.at[own], wg3.at[own], g3_s.at[i], g3_r.at[back], qdev(i))
        c.start()
        g3_copies.append(c)

    total = dqacc[0] * (DH**-0.5)
    for i in range(1, NQ):
        rcopy(dqsend.at[i], dqrecv.at[i], dq_s.at[i], dq_r.at[i], partner).wait_recv()
        total = total + dqrecv[i].astype(F32)
    dq_ref[...] = total

    total = dkacc[...]
    for j in range(1, NB):
        rcopy(dsend.at[j], drecv.at[j], dk_s.at[j], dk_r.at[j], partner).wait_recv()
        total = total + drecv[j].astype(F32)
    dkv_ref[...] = total * live_col

    for i in range(1, NQ):
        rcopy(wg3.at[0], wg3.at[0], g3_s.at[i], g3_r.at[i], partner).wait_recv()
    for s in range(NQ):
        wg_ref[s * RW : (s + 1) * RW, :] = wg3[s].astype(F32)

    for c in (
        kv_copies + q_copies + w_copies + st_copies + o_copies + at_copies + g1_copies + dq_copies + g2_copies + g3_copies
    ):
        c.wait_send()
    for j in range(1, NB):
        rcopy(dsend.at[j], drecv.at[j], dk_s.at[j], dk_r.at[j], partner).wait_send()


def solution(mesh):
    NMP = mesh.shape["mp"]
    NSEQ = mesh.shape["seq"]
    NY, NZ = {64: (4, 8), 8: (2, 2), 16: (2, 4)}[NSEQ]
    NB, NQ = NZ, NY * CORES
    U = NQ // 2

    def shards(queries, key_value, tile_fill, out_weight, grad_output):
        T = queries.shape[0]
        D = out_weight.shape[2]
        qT = queries[:, 0, :].T
        kv = key_value[:, 0, :]
        w = out_weight[0]
        V = pl.BlockSpec(memory_space=pltpu.VMEM)
        v = pltpu.VMEM
        dma = lambda n: pltpu.SemaphoreType.DMA((n,))
        RW = DH // NQ
        scratch = [
            v((NB, T + 16, 2 * DH), BF), v((NB, 2 * DH + 16, T), BF), v((NQ, 2 * DH, T), BF), v((NQ, 2 * DH, T), BF),
            v((NQ, DH, T), BF), v((NB, NQ, T, T), BF), v((NB, NQ, 8, T), F32), v((NQ, 8, T), F32),
            v((NQ, DH + 16, T), F32), v((2, U, 8, T), F32),
            v((U, T, T), F32), v((U, T, T), F32), v((U, 2 * DH, T), BF), v((U, 2 * DH, T), BF),
            v((U, T, T), BF), v((U, T, T), BF),
            v((2 * NQ, T), F32), v((NQ, 2 * NQ, T), F32), v((NQ + 1, 8, T), F32), v((NQ + 1, 8, T), F32),
            v((NQ, DH, T), BF), v((NQ, DH, T), BF), v((T, 2 * DH), F32), v((NB, T, 2 * DH), BF), v((NB, T, 2 * DH), BF),
            v((NQ, DH, T), F32), v((NQ, DH, T), BF), v((NQ, DH, T), BF),
            v((T, D), BF), v((NMP, DH, D), BF), v((NMP, DH, T), BF),
            v((NQ, RW, D), BF), v((NQ, RW, D), BF), v((NZ, RW, D), BF), v((NQ, RW, D), BF),
            dma(NB), dma(NB), dma(NQ), dma(NQ), dma(NQ), dma(NQ), dma(NQ), dma(NQ), dma(NQ),
            dma(NB), dma(NB), dma(NQ), dma(NQ),
            dma(NMP), dma(NMP), dma(NMP), dma(NMP), dma(NQ), dma(NQ), dma(NZ), dma(NZ), dma(NQ), dma(NQ),
        ]
        out, dqT, dkv, wg = pl.pallas_call(
            functools.partial(kernel, NY, NZ, NMP),
            name="voxel_attention",
            out_shape=[
                jax.ShapeDtypeStruct((T, D), BF),
                jax.ShapeDtypeStruct((DH, T), F32),
                jax.ShapeDtypeStruct((T, 2 * DH), F32),
                jax.ShapeDtypeStruct((DH, D), F32),
            ],
            in_specs=[pl.BlockSpec(memory_space=pltpu.SMEM), V, V, V, V],
            out_specs=[V, V, V, V],
            scratch_shapes=scratch,
            compiler_params=pltpu.CompilerParams(
                collective_id=0, has_side_effects=True, vmem_limit_bytes=60 * 1024 * 1024
            ),
        )(tile_fill, qT, kv, w, grad_output)
        return out, dqT.T[:, None, :], dkv[:, None, :], wg[None]

    return jax.shard_map(
        shards,
        mesh=mesh,
        in_specs=(
            P("seq", "mp", None),
            P("seq", "mp", None),
            P("seq"),
            P("mp", None, None),
            P("seq", None),
        ),
        out_specs=(P("seq", None), P("seq", "mp", None), P("seq", "mp", None), P("mp", None, None)),
        check_vma=False,
    )
```

```python
import functools

import jax
import jax.numpy as jnp
from jax import lax
from jax.experimental import pallas as pl
from jax.experimental.pallas import tpu as pltpu
from jax.sharding import PartitionSpec as P

MESH = pl.DeviceIdType.MESH
BF = jnp.bfloat16
F32 = jnp.float32
TILE = 128
DH = 64
CORES = 2


def nn(a, b):
    return jnp.dot(a, b, preferred_element_type=F32)


def nt(a, b):
    return lax.dot_general(a, b, (((1,), (1,)), ((), ())), preferred_element_type=F32)


def place(offset, size):
    o = offset % size
    if o > size // 2:
        o -= size
    return 2 * o - 1 if o > 0 else -2 * o


def offset_of(rank):
    half = (rank + 1) // 2
    return half if rank % 2 == 1 else -half


def kernel(
    NY, NZ, NMP,
    fill_hbm, qT_hbm, kv_hbm, w_hbm, g_hbm,
    out_ref, dq_ref, dkv_ref, wg_ref,
    fill_ref, qT_ref, kv_ref, g_ref, in_sem,
    kvb, kvT, qq, dd, qS, p, mh, m, oacc, ab, ds,
    sA, sB, Ll, Dl, rr, wq,
    stl, str_, Lg, Dg, osend, orecv, dkp, dsend, drecv, dqacc, dqsend, dqrecv,
    gmb, wall, attall, wg1s, wg1r, wg2, wg3,
    kv0_s, kv_s, kv_r, q_s, q_r, ql_s, d_s, d_r, dl_s, st_s, st_r, o_s, o_r, dk_s, dk_r, dq_s, dq_r,
    w_s, w_r, wl_s, wl_r, at_s, at_r, g1_s, g1_r, g2_s, g2_r, g3_s, g3_r,
):
    T = kv_ref.shape[0]
    D = wall.shape[3]
    NB, NQ = NZ, NY * CORES
    U = NQ // 2
    H = NB // 2
    RW = DH // NQ
    YL = 2 if NMP % 2 == 0 else 1
    X = NMP // YL
    CUTS = ((0, 144), (144, 128))
    SCALE = DH**-0.5

    seq = lax.axis_index("seq")
    mp = lax.axis_index("mp")
    core = seq % CORES
    z = (seq // CORES) % NZ
    y = seq // (CORES * NZ)

    def zdev(o):
        return ((y * NZ + (z + o + NZ) % NZ) * CORES + core, mp)

    def qoff(i):
        return offset_of(i // 2) % NY, i % 2

    def qdev(i):
        dy, dc = qoff(i)
        return ((((y + dy) % NY) * NZ + z) * CORES + (core + dc) % 2, mp)

    def qabs(i):
        dy, dc = qoff(i)
        return ((y + dy) % NY) * CORES + (core + dc) % 2

    def qback(i):
        dy, dc = qoff(i)
        return 2 * place(-dy, NY) + dc

    def mdev(r):
        return (seq, (mp + r) % NMP)

    def head_at(flip, dx):
        return ((mp // X + flip) % YL) * X + (mp % X + dx + X) % X

    partner = qdev(1)

    def rcopy(src, dst, ssem, rsem, dev):
        return pltpu.make_async_remote_copy(
            src_ref=src, dst_ref=dst, send_sem=ssem, recv_sem=rsem, device_id=dev, device_id_type=MESH
        )

    barrier = pltpu.get_barrier_semaphore()
    for j in range(1, NB):
        pl.semaphore_signal(barrier, inc=1, device_id=zdev(offset_of(j)), device_id_type=MESH)
    for i in range(1, NQ):
        pl.semaphore_signal(barrier, inc=1, device_id=qdev(i), device_id_type=MESH)
    for r in range(1, NMP):
        pl.semaphore_signal(barrier, inc=1, device_id=mdev(r), device_id_type=MESH)

    w_ref = wall.at[mp]
    loads = [
        pltpu.make_async_copy(a, b, in_sem.at[n])
        for n, (a, b) in enumerate(((kv_hbm, kv_ref), (qT_hbm, qT_ref), (w_hbm, w_ref), (g_hbm, g_ref), (fill_hbm, fill_ref)))
    ]
    for c in loads:
        c.start()

    rows = lax.broadcasted_iota(jnp.int32, (T, 1), 0)
    loads[4].wait()
    fills = [fill_ref[t] for t in range(T // TILE)]
    live_col = jnp.zeros((T, 1), F32)
    for t in range(T // TILE):
        inside = (rows >= t * TILE) & (rows < t * TILE + fills[t])
        live_col = jnp.where(inside, 1.0, live_col)
    lanes = lax.broadcasted_iota(jnp.int32, (1, T), 1)
    live_row = jnp.zeros((1, T), F32)
    for t in range(T // TILE):
        inside = (lanes >= t * TILE) & (lanes < t * TILE + fills[t])
        live_row = jnp.where(inside, 1.0, live_row)
    loads[0].wait()
    kv = kv_ref[...].astype(F32)
    is_key = lax.broadcasted_iota(jnp.int32, (1, 2 * DH), 1) < DH
    stand_in = jnp.where(is_key, kv[0:1, :], 0.0)
    kvb[0, 0:T, :] = jnp.where(live_col > 0.0, kv, stand_in).astype(BF)
    tail_rows = lax.broadcasted_iota(jnp.int32, (16, 1), 0)
    tail = jnp.zeros((16, TILE), F32)
    for t in range(T // TILE):
        tail = jnp.where(tail_rows == t, live_row[:, t * TILE : (t + 1) * TILE], tail)
    kvb[0, T : T + 16, :] = tail.astype(BF)
    loads[1].wait()
    qq[0] = (qT_ref[...].astype(F32) * SCALE).astype(BF)
    loads[2].wait()
    loads[3].wait()
    gmb[...] = (g_ref[...].astype(F32) * live_col).astype(BF)
    dd[0] = nt(wall[mp].reshape(DH, D), gmb[...]).astype(BF)

    def prepare_keys(j):
        live16 = kvb[j, T : T + 16, :].astype(F32)
        row = jnp.concatenate([live16[t : t + 1, :] for t in range(T // TILE)], axis=1)
        kvT[j, 0 : 2 * DH, :] = (kvb[j, 0:T, :].astype(F32).T * row).astype(BF)
        kvT[j, 2 * DH : 2 * DH + 16, :] = jnp.broadcast_to(row, (16, T)).astype(BF)

    def prepare_queries(i):
        qS[i, 0:DH, :] = qq[i]

    prepare_keys(0)
    prepare_queries(0)
    for i in range(NQ):
        qS[i, DH : 2 * DH, :] = jnp.zeros((DH, T), BF)
        wq[i, DH : 2 * DH, :] = jnp.zeros((DH, T), BF)

    pl.semaphore_wait(barrier, (NB - 1) + (NQ - 1) + (NMP - 1))

    copies = []

    def send(src, dst, ssem, rsem, dev):
        rcopy(src, dst, ssem, rsem, dev).start()
        copies.append(lambda: (src, ssem))

    def send_row(buf, a, b, ssem, k, rsem, dev):
        rcopy(buf.at[a], buf.at[b], ssem.at[k], rsem, dev).start()
        copies.append(lambda: (buf.at[(0, 0) if isinstance(a, tuple) else 0], ssem.at[k]))

    def arrive(dst, rsem):
        rcopy(dst, dst, kv0_s.at[0], rsem, partner).wait_recv()

    def send_keys(j, hf, to, sem, k, dev):
        lo, size = CUTS[hf]
        src, dst = kvb.at[j, pl.ds(lo, size)], kvb.at[to, pl.ds(lo, size)]
        rcopy(src, dst, sem.at[k], kv_r.at[2 * to + hf], dev).start()
        copies.append(lambda: (kvb.at[0, pl.ds(lo, size)], sem.at[k]))

    right = place(-1, NZ)
    for hf in range(2):
        if NZ > 2 or hf == 0:
            send_keys(0, hf, right, kv0_s, hf, zdev(1))
        if NZ > 2 or hf == 1:
            send_keys(0, hf, 1, kv0_s, 2 + hf, zdev(-1))

    def spread(buf, ssem, rsem):
        for k in range(1, NY):
            i, back = 2 * k, qback(2 * k)
            send(buf.at[0], buf.at[back], ssem.at[i], rsem.at[back], qdev(i))
        send(buf.at[0], buf.at[1], ssem.at[1], rsem.at[1], partner)

    spread(qq, q_s, q_r)
    spread(dd, d_s, d_r)
    if YL == 2:
        send_row(wall, (mp, core), (mp, core), w_s, 0, w_r.at[0], (seq, head_at(1, 0)))
    for i in range(NQ):
        m[i] = jnp.full((8, T), -1e30, F32)
        oacc[i] = jnp.zeros((2 * DH + 16, T), F32)
        dqacc[i] = jnp.zeros((DH, T), F32)

    def relay(buf, lsem, rsem, k):
        i = 2 * k
        arrive(buf.at[i], rsem.at[i])
        send_row(buf, i, i + 1, lsem, i, rsem.at[i + 1], partner)

    def forward_keys(j, hf):
        arrive(kvb.at[j, pl.ds(*CUTS[hf])], kv_r.at[2 * j + hf])
        k = (j + 1) // 2
        odd = j % 2 == 1
        if j < NZ - 1 and (k + 1 < NZ // 2 or hf == (1 if odd else 0)):
            to = j + 2 if k + 1 < NZ // 2 else NZ - 1
            send_keys(j, hf, to, kv_s, 2 * j + hf, zdev(-1 if odd else 1))

    def before(it):
        def take(js):
            for hf in range(2):
                for j in js:
                    forward_keys(j, hf)

        js = []
        if it == 0 and H > 1:
            js = [1, 2]
        if it > 1 and it + 1 < H:
            js = [2 * it + 1, 2 * it + 2]
        if it == NB - 1:
            js = [NB - 1]
        take(js)
        if it == 0:
            for k in range(1, max(NY - 1, 1)):
                relay(qq, ql_s, q_r, k)
        for half in range(2):
            if it == half * (H // 2):
                if half == 1 and it == 0:
                    relay(qq, ql_s, q_r, NY - 1)
                for i in range(half * U, half * U + U):
                    if i % 2 == 1:
                        arrive(qq.at[i], q_r.at[i])
                    if i > 0:
                        prepare_queries(i)
        if it == 0 and H > 2:
            take([3, 4])
            js = js + [3, 4]
        if it == 0 and H // 2 > 0:
            relay(qq, ql_s, q_r, NY - 1)
        for j in js:
            prepare_keys(j)
        if it == max(NB - 5, 0):
            if YL == 2:
                arrive(wall.at[0, 0], w_r.at[0])
            for dx in range(1, X):
                for flip in range(YL):
                    k = 1 + 2 * (dx - 1) + flip
                    h = head_at(flip, 0)
                    send_row(wall, (h, core), (h, core), w_s, k, w_r.at[k], (seq, head_at(0, dx)))
        if it == max(NB - 2, 0):
            for k in range(1, NY):
                relay(dd, dl_s, d_r, k)

    def step_of(n):
        late = n - 2 * H
        if isinstance(n, int):
            j = n if n < H else (n - H if late < 0 else H + late // 2)
            return j, U * (0 if n < H else (1 if late < 0 else late % 2))
        j = jnp.where(n < H, n, jnp.where(late < 0, n - H, H + jnp.right_shift(late, 1)))
        half = jnp.where(n < H, 0, jnp.where(late < 0, 1, late & 1))
        return j, half * U

    def S(n, buf):
        j, i0 = step_of(n)
        for t in range(U):
            buf[t] = nn(kvb[j, 0:T, :], qS[i0 + t])

    def E(n, buf, par):
        j, i0 = step_of(n)
        for t in range(U):
            i = i0 + t
            m_old = m[i, 0:1, :]
            m_new = jnp.maximum(m_old, jnp.max(buf[t], axis=0, keepdims=True))
            mh[j, i, 0:1, :] = m_new
            m[i, 0:1, :] = m_new
            ab[par, t, 0:1, :] = jnp.exp(m_old - m_new)
            p[j, i] = jnp.exp(buf[t] - m_new).astype(BF)

    def O(n, par):
        j, i0 = step_of(n)
        for t in range(U):
            i = i0 + t
            oacc[i] = oacc[i] * ab[par, t, 0:1, :] + nn(kvT[j], p[j, i])

    before(0)
    first, last = 0, 2 * NB - 1
    S(first, sA)
    E(first, sA, 0)
    S(first + 1, sB)

    @pl.loop(1, NB)
    def _(it):
        for fixed in range(1, NB):
            if fixed in WAITS(NB, H):
                pl.when(it == fixed)(functools.partial(before, fixed))
        n = 2 * it
        S(n, sA)
        E(n - 1, sB, 1)
        O(n - 2, 0)
        S(n + 1, sB)
        E(n, sA, 0)
        O(n - 1, 1)

    E(last, sB, 1)
    O(last - 1, 0)
    O(last, 1)
    for k in range(NY):
        arrive(dd.at[2 * k + 1], d_r.at[2 * k + 1])

    for i in range(NQ):
        total = oacc[i, 2 * DH : 2 * DH + 1, :]
        inv = 1.0 / total
        o = oacc[i, DH : 2 * DH, :] * inv
        oacc[i, 0:DH, :] = oacc[i, 0:DH, :] * inv
        osend[i] = o.astype(BF)
        lrow = m[i, 0:1, :] + jnp.log(total)
        drow = jnp.sum(o * dd[i].astype(F32), axis=0, keepdims=True)
        Ll[i, 0:1, :] = lrow
        Dl[i, 0:1, :] = drow
        stl[pl.ds(qabs(i), 1), :] = lrow
        stl[pl.ds(NQ + qabs(i), 1), :] = drow

    for i in range(1, NQ):
        back = qback(i)
        send(stl, str_.at[back], st_s.at[i], st_r.at[back], qdev(i))
    for i in range(1, NQ):
        back = qback(i)
        send(osend.at[i], orecv.at[back], o_s.at[i], o_r.at[back], qdev(i))

    def Ust(j, half, buf):
        for t in range(U):
            i = half * U + t
            c = jnp.exp(mh[j, i, 0:1, :] - Ll[i, 0:1, :])
            rhs = jnp.concatenate([jnp.zeros((DH, T), BF), (dd[i].astype(F32) * c).astype(BF)], axis=0)
            buf[t] = nn(kvb[j, 0:T, :], rhs) - c * Dl[i, 0:1, :]

    def Dst(j, half, buf):
        for t in range(U):
            i = half * U + t
            ds[j, i] = (p[j, i].astype(F32) * buf[t]).astype(BF)

    def Mst(j, half):
        for t in range(U):
            i = half * U + t
            dqacc[i] += nn(kvT[j, 0:DH, :], ds[j, i])

    Ust(0, 0, sA)
    Dst(0, 0, sA)
    Ust(0, 1, sB)

    @pl.loop(1, NB)
    def _(j):
        Ust(j, 0, sA)
        Dst(j - 1, 1, sB)
        Mst(j - 1, 0)
        Ust(j, 1, sB)
        Dst(j, 0, sA)
        Mst(j - 1, 1)

    Dst(NB - 1, 1, sB)
    Mst(NB - 1, 0)
    Mst(NB - 1, 1)

    str_[0] = stl[...]
    for i in range(1, NQ):
        arrive(str_.at[i], st_r.at[i])
    if YL == 2:
        send_row(wall, (head_at(1, 0), core), (head_at(1, 0), core), wl_s, 0, wl_r.at[0], partner)
    for dx in range(1, X):
        for flip in range(YL):
            k = 1 + 2 * (dx - 1) + flip
            h = head_at(flip, -dx)
            arrive(wall.at[0, 0], w_r.at[k])
            send_row(wall, (h, core), (h, core), wl_s, k, wl_r.at[k], partner)
    big = str_[0, 0:NQ, :]
    for s in range(1, NQ):
        big = jnp.maximum(big, str_[s, 0:NQ, :])
    wsum = jnp.zeros((NQ, T), F32)
    dsum = jnp.zeros((NQ, T), F32)
    for s in range(NQ):
        wt = jnp.exp(str_[s, 0:NQ, :] - big)
        wsum = wsum + wt
        dsum = dsum + wt * str_[s, NQ : 2 * NQ, :]
    Lg[0:NQ, :] = big + jnp.log(wsum)
    Dg[0:NQ, :] = dsum / wsum
    for i in range(NQ):
        w = jnp.exp(Ll[i, 0:1, :] - Lg[pl.ds(qabs(i), 1), :])
        e = w * (Dl[i, 0:1, :] - Dg[pl.ds(qabs(i), 1), :])
        q32 = qq[i].astype(F32)
        wq[i, 0:DH, :] = (q32 * w).astype(BF)
        rr[i, 0:DH, :] = q32 * e
        rr[i, DH : 2 * DH, :] = dd[i].astype(F32) * w
        total = (dqacc[i] * w + oacc[i, 0:DH, :] * e) * SCALE
        if i == 0:
            dqacc[0] = total
        else:
            dqsend[i] = total.astype(BF)

    def key_pair(n):
        @pl.loop(0, 2)
        def _(b):
            j = NB - 1 - 2 * n - b
            acc = None
            for i in range(NQ):
                c = jnp.exp(mh[j, i, 0:1, :] - Ll[i, 0:1, :])
                r = nt(ds[j, i], wq[i]) + nt(p[j, i], (rr[i] * c).astype(BF))
                acc = r if acc is None else acc + r
            dkp[j] = acc

    def pass_on(j, hf):
        lo, size = hf * (T // 2), T // 2
        total = dkp[j, pl.ds(lo, size), :]
        odd = j % 2 == 1
        if j < NZ - 3 or (j == NZ - 3 and hf == 0) or (j == NZ - 2 and hf == 1):
            arrive(drecv.at[j, pl.ds(lo, size)], dk_r.at[2 * j + hf])
            total = total + drecv[j, pl.ds(lo, size), :].astype(F32)
        dsend[j, pl.ds(lo, size), :] = total.astype(BF)
        if j == NZ - 1:
            onward = hf == 0
            to = max(NZ - 3, 0) if hf == 0 else max(NZ - 2, 1)
        else:
            onward = odd
            to = j - 2 if j >= 3 else (0 if j == 1 else NZ - 1)
        send(dsend.at[j, pl.ds(lo, size)], drecv.at[to, pl.ds(lo, size)], dk_s.at[2 * j + hf], dk_r.at[2 * to + hf],
             zdev(1 if onward else -1))

    def attended_rows():
        for i in range(1, NQ):
            arrive(orecv.at[i], o_r.at[i])
        orecv[0] = osend[0]
        own = Lg[pl.ds(qabs(0), 1), :]
        att = jnp.zeros((DH, T), F32)
        for s in range(NQ):
            att = att + jnp.exp(str_[s, pl.ds(qabs(0), 1), :] - own) * orecv[s].astype(F32)
        wgp = nn(att.astype(BF), gmb[...])
        for s in range(NQ):
            wg1s[s] = wgp[s * RW : (s + 1) * RW, :].astype(BF)
        for i in range(1, NQ):
            back = qback(i)
            send(wg1s.at[qabs(i)], wg1r.at[back], g1_s.at[i], g1_r.at[back], qdev(i))
        attall[mp] = (att * live_row).astype(BF)
        for r in range(1, NMP):
            send(attall.at[mp], attall.at[mp], at_s.at[r], at_r.at[r], mdev(r))

    def gradient_over_z():
        wg1r[0] = wg1s[qabs(0)]
        for i in range(1, NQ):
            arrive(wg1r.at[i], g1_r.at[i])
        part = wg1r[0].astype(F32)
        for i in range(1, NQ):
            part = part + wg1r[i].astype(F32)
        wg2[z] = part.astype(BF)
        for r in range(1, NZ):
            send(wg2.at[z], wg2.at[z], g2_s.at[r], g2_r.at[r], zdev(r))

    for n in range(H):
        key_pair(n)
        j = NB - 1 - 2 * n
        pass_on(j, 0)
        if n > 0:
            pass_on(j + 1, 1)
        pass_on(j, 1)
        if j > 1:
            pass_on(j - 1, 0)
        if n == max(H - 2, 0) and n > 0:
            gradient_over_z()
        if n == 0:
            attended_rows()
            for i in range(1, NQ):
                back = qback(i)
                send(dqsend.at[i], dqrecv.at[back], dq_s.at[i], dq_r.at[back], qdev(i))

    if H <= 2:
        gradient_over_z()

    for r in range(1, NMP):
        arrive(wall.at[0, 0], wl_r.at[r - 1])
        arrive(attall.at[0], at_r.at[r])
    att_rows = attall[...].reshape(NMP * DH, T).astype(F32).T.astype(BF)
    out_ref[...] = nn(att_rows, wall[...].reshape(NMP * DH, D)).astype(BF)

    total = dqacc[0]
    for i in range(1, NQ):
        arrive(dqrecv.at[i], dq_r.at[i])
        total = total + dqrecv[i].astype(F32)
    dq_ref[...] = total

    for hf in range(2):
        rows_of = pl.ds(hf * (T // 2), T // 2)
        total = dkp[0, rows_of, :]
        for slot in (0, NB - 1):
            if NZ > 2 or slot == hf:
                arrive(drecv.at[slot, rows_of], dk_r.at[2 * slot + hf])
                total = total + drecv[slot, rows_of, :].astype(F32)
        dkv_ref[rows_of, :] = total * live_col[hf * (T // 2) : (hf + 1) * (T // 2), :]

    for r in range(1, NZ):
        arrive(wg2.at[0], g2_r.at[r])
    part = wg2[0].astype(F32)
    for k in range(1, NZ):
        part = part + wg2[k].astype(F32)
    own = qabs(0)
    wg3[own] = part.astype(BF)
    for i in range(1, NQ):
        send(wg3.at[own], wg3.at[own], g3_s.at[i], g3_r.at[qback(i)], qdev(i))
    for i in range(1, NQ):
        arrive(wg3.at[0], g3_r.at[i])
    for s in range(NQ):
        wg_ref[s * RW : (s + 1) * RW, :] = wg3[s].astype(F32)

    for make in copies:
        src, ssem = make()
        rcopy(src, src, ssem, kv_r.at[0], partner).wait_send()


def WAITS(NB, H):
    return set(range(1, H - 1)) | {H // 2, NB - 1, max(NB - 5, 0), max(NB - 2, 0)}


def write_out(a_ref, b_ref, c_ref, d_ref, a_hbm, b_hbm, c_hbm, d_hbm, sem):
    pairs = ((a_ref, a_hbm), (b_ref, b_hbm), (c_ref, c_hbm), (d_ref, d_hbm))
    copies = [pltpu.make_async_copy(r, h, sem.at[n]) for n, (r, h) in enumerate(pairs)]
    for c in copies:
        c.start()
    for c in copies:
        c.wait()


def solution(mesh):
    NMP = mesh.shape["mp"]
    NSEQ = mesh.shape["seq"]
    NY, NZ = {64: (4, 8), 8: (2, 2), 16: (2, 4)}[NSEQ]
    NB, NQ = NZ, NY * CORES
    U = NQ // 2

    def shards(queries, key_value, tile_fill, out_weight, grad_output):
        T = queries.shape[0]
        D = out_weight.shape[2]
        qT = queries[:, 0, :].T
        kv = key_value[:, 0, :]
        w = out_weight.reshape(CORES, DH // CORES, out_weight.shape[2])
        V = pl.BlockSpec(memory_space=pltpu.VMEM)
        A = pl.BlockSpec(memory_space=pl.ANY)
        v = pltpu.VMEM
        dma = lambda n: pltpu.SemaphoreType.DMA((n,))
        RW = DH // NQ
        scratch = [
            pltpu.SMEM((T // TILE,), jnp.int32), v((DH, T), BF), v((T, 2 * DH), BF), v((T, D), BF), dma(5),
            v((NB, T + 16, 2 * DH), BF), v((NB, 2 * DH + 16, T), BF), v((NQ, DH, T), BF), v((NQ, DH, T), BF),
            v((NQ, 2 * DH, T), BF), v((NB, NQ, T, T), BF), v((NB, NQ, 8, T), F32), v((NQ, 8, T), F32),
            v((NQ, 2 * DH + 16, T), F32), v((2, U, 8, T), F32), v((NB, NQ, T, T), BF),
            v((U, T, T), F32), v((U, T, T), F32), v((NQ, 8, T), F32), v((NQ, 8, T), F32),
            v((NQ, 2 * DH, T), F32), v((NQ, 2 * DH, T), BF),
            v((2 * NQ, T), F32), v((NQ, 2 * NQ, T), F32), v((8, T), F32), v((8, T), F32),
            v((NQ, DH, T), BF), v((NQ, DH, T), BF), v((NB, T, 2 * DH), F32), v((NB, T, 2 * DH), BF), v((NB, T, 2 * DH), BF),
            v((NQ, DH, T), F32), v((NQ, DH, T), BF), v((NQ, DH, T), BF),
            v((T, D), BF), v((NMP, CORES, DH // CORES, D), BF), v((NMP, DH, T), BF),
            v((NQ, RW, D), BF), v((NQ, RW, D), BF), v((NZ, RW, D), BF), v((NQ, RW, D), BF),
            dma(4), dma(2 * NB), dma(2 * NB), dma(NQ), dma(NQ), dma(NQ), dma(NQ), dma(NQ), dma(NQ), dma(NQ), dma(NQ),
            dma(NQ), dma(NQ), dma(2 * NB), dma(2 * NB), dma(NQ), dma(NQ),
            dma(NMP), dma(NMP), dma(NMP), dma(NMP), dma(NMP), dma(NMP), dma(NQ), dma(NQ), dma(NZ), dma(NZ), dma(NQ), dma(NQ),
        ]
        shapes = [((T, D), BF), ((DH, T), F32), ((T, 2 * DH), F32), ((DH, D), F32)]
        results = pl.pallas_call(
            functools.partial(kernel, NY, NZ, NMP),
            name="voxel_attention",
            out_shape=[pltpu.VMEM(*s) for s in shapes],
            in_specs=[A, A, A, A, A],
            out_specs=[V, V, V, V],
            scratch_shapes=scratch,
            compiler_params=pltpu.CompilerParams(
                collective_id=0, has_side_effects=True, vmem_limit_bytes=56 * 1024 * 1024
            ),
        )(tile_fill, qT, kv, w, grad_output)
        out, dqT, dkv, wg = pl.pallas_call(
            write_out,
            name="write_out",
            out_shape=[jax.ShapeDtypeStruct(*s) for s in shapes],
            in_specs=[V, V, V, V],
            out_specs=[A, A, A, A],
            scratch_shapes=[dma(4)],
        )(*(pltpu.with_memory_space_constraint(r, pltpu.VMEM) for r in results))
        return out, dqT.T[:, None, :], dkv[:, None, :], wg[None]

    return jax.shard_map(
        shards,
        mesh=mesh,
        in_specs=(
            P("seq", "mp", None),
            P("seq", "mp", None),
            P("seq"),
            P("mp", None, None),
            P("seq", None),
        ),
        out_specs=(P("seq", None), P("seq", "mp", None), P("seq", "mp", None), P("mp", None, None)),
        check_vma=False,
    )
```

```python
import functools

import jax
import jax.numpy as jnp
from jax import lax
from jax.experimental import pallas as pl
from jax.experimental.pallas import tpu as pltpu
from jax.sharding import PartitionSpec as P

MESH = pl.DeviceIdType.MESH
BF = jnp.bfloat16
F32 = jnp.float32
TILE = 128
DH = 64
CORES = 2


def nn(a, b):
    return jnp.dot(a, b, preferred_element_type=F32)


def nt(a, b):
    return lax.dot_general(a, b, (((1,), (1,)), ((), ())), preferred_element_type=F32)


def place(offset, size):
    o = offset % size
    if o > size // 2:
        o -= size
    return 2 * o - 1 if o > 0 else -2 * o


def offset_of(rank):
    half = (rank + 1) // 2
    return half if rank % 2 == 1 else -half


def kernel(
    NY, NZ, NMP,
    fill_hbm, qT_hbm, kv_hbm, w_hbm, g_hbm,
    out_ref, dq_ref, dkv_ref, wg_ref,
    fill_ref, qT_ref, kv_ref, g_ref, in_sem,
    kvb, kvT, qq, dd, qS, p, mh, m, oacc, ab, ds,
    sA, sB, Ll, Dl, rr, wq,
    stl, pst, str_, wpair, Lg, Dg, osend, opair, orecv, dkp, dsend, drecv, dqacc, dqsend, dqpair, dqrecv,
    gmb, wall, attall, wg1s, wg1r, wg2, wg3,
    kv0_s, kv_s, kv_r, q_s, q_r, ql_s, d_s, d_r, dl_s, st_s, st_r, o_s, o_r, dk_s, dk_r, dq_s, dq_r,
    w_s, w_r, wl_s, wl_r, at_s, at_r, g1_s, g1_r, g2_s, g2_r, g3_s, g3_r,
):
    T = kv_ref.shape[0]
    D = wall.shape[3]
    NB, NQ = NZ, NY * CORES
    U = NQ // 2
    H = NB // 2
    RW = DH // NQ
    YL = 2 if NMP % 2 == 0 else 1
    X = NMP // YL
    CUTS = ((0, 144), (144, 128))
    SCALE = DH**-0.5

    seq = lax.axis_index("seq")
    mp = lax.axis_index("mp")
    core = seq % CORES
    z = (seq // CORES) % NZ
    y = seq // (CORES * NZ)

    def zdev(o):
        return ((y * NZ + (z + o + NZ) % NZ) * CORES + core, mp)

    def qoff(i):
        return offset_of(i // 2) % NY, i % 2

    def qdev(i):
        dy, dc = qoff(i)
        return ((((y + dy) % NY) * NZ + z) * CORES + (core + dc) % 2, mp)

    def qabs(i):
        dy, dc = qoff(i)
        return ((y + dy) % NY) * CORES + (core + dc) % 2

    def qback(i):
        dy, dc = qoff(i)
        return 2 * place(-dy, NY) + dc

    def mdev(r):
        return (seq, (mp + r) % NMP)

    def head_at(flip, dx):
        return ((mp // X + flip) % YL) * X + (mp % X + dx + X) % X

    partner = qdev(1)

    def rcopy(src, dst, ssem, rsem, dev):
        return pltpu.make_async_remote_copy(
            src_ref=src, dst_ref=dst, send_sem=ssem, recv_sem=rsem, device_id=dev, device_id_type=MESH
        )

    barrier = pltpu.get_barrier_semaphore()
    for j in range(1, NB):
        pl.semaphore_signal(barrier, inc=1, device_id=zdev(offset_of(j)), device_id_type=MESH)
    for i in range(1, NQ):
        pl.semaphore_signal(barrier, inc=1, device_id=qdev(i), device_id_type=MESH)
    for r in range(1, NMP):
        pl.semaphore_signal(barrier, inc=1, device_id=mdev(r), device_id_type=MESH)

    w_ref = wall.at[mp]
    loads = [
        pltpu.make_async_copy(a, b, in_sem.at[n])
        for n, (a, b) in enumerate(((kv_hbm, kv_ref), (qT_hbm, qT_ref), (w_hbm, w_ref), (g_hbm, g_ref), (fill_hbm, fill_ref)))
    ]
    for c in loads:
        c.start()

    rows = lax.broadcasted_iota(jnp.int32, (T, 1), 0)
    loads[4].wait()
    fills = [fill_ref[t] for t in range(T // TILE)]
    live_col = jnp.zeros((T, 1), F32)
    for t in range(T // TILE):
        inside = (rows >= t * TILE) & (rows < t * TILE + fills[t])
        live_col = jnp.where(inside, 1.0, live_col)
    lanes = lax.broadcasted_iota(jnp.int32, (1, T), 1)
    live_row = jnp.zeros((1, T), F32)
    for t in range(T // TILE):
        inside = (lanes >= t * TILE) & (lanes < t * TILE + fills[t])
        live_row = jnp.where(inside, 1.0, live_row)
    loads[0].wait()
    kv = kv_ref[...].astype(F32)
    is_key = lax.broadcasted_iota(jnp.int32, (1, 2 * DH), 1) < DH
    stand_in = jnp.where(is_key, kv[0:1, :], 0.0)
    kvb[0, 0:T, :] = jnp.where(live_col > 0.0, kv, stand_in).astype(BF)
    tail_rows = lax.broadcasted_iota(jnp.int32, (16, 1), 0)
    tail = jnp.zeros((16, TILE), F32)
    for t in range(T // TILE):
        tail = jnp.where(tail_rows == t, live_row[:, t * TILE : (t + 1) * TILE], tail)
    kvb[0, T : T + 16, :] = tail.astype(BF)
    loads[1].wait()
    qq[0] = (qT_ref[...].astype(F32) * SCALE).astype(BF)

    def prepare_keys(j):
        live16 = kvb[j, T : T + 16, :].astype(F32)
        row = jnp.concatenate([live16[t : t + 1, :] for t in range(T // TILE)], axis=1)
        kvT[j, 0 : 2 * DH, :] = (kvb[j, 0:T, :].astype(F32).T * row).astype(BF)
        kvT[j, 2 * DH : 2 * DH + 16, :] = jnp.broadcast_to(row, (16, T)).astype(BF)

    def prepare_queries(i):
        qS[i, 0:DH, :] = qq[i]

    pl.semaphore_wait(barrier, (NB - 1) + (NQ - 1) + (NMP - 1))

    copies = []

    def send(src, dst, ssem, rsem, dev):
        rcopy(src, dst, ssem, rsem, dev).start()
        copies.append(lambda: (src, ssem))

    def send_row(buf, a, b, ssem, k, rsem, dev):
        rcopy(buf.at[a], buf.at[b], ssem.at[k], rsem, dev).start()
        copies.append(lambda: (buf.at[(0, 0) if isinstance(a, tuple) else 0], ssem.at[k]))

    def arrive(dst, rsem):
        rcopy(dst, dst, kv0_s.at[0], rsem, partner).wait_recv()

    def send_keys(j, hf, to, sem, k, dev):
        lo, size = CUTS[hf]
        src, dst = kvb.at[j, pl.ds(lo, size)], kvb.at[to, pl.ds(lo, size)]
        rcopy(src, dst, sem.at[k], kv_r.at[2 * to + hf], dev).start()
        copies.append(lambda: (kvb.at[0, pl.ds(lo, size)], sem.at[k]))

    right = place(-1, NZ)
    for hf in range(2):
        if NZ > 2 or hf == 0:
            send_keys(0, hf, right, kv0_s, hf, zdev(1))
        if NZ > 2 or hf == 1:
            send_keys(0, hf, 1, kv0_s, 2 + hf, zdev(-1))

    def spread(buf, ssem, rsem):
        for k in range(1, NY):
            i, back = 2 * k, qback(2 * k)
            send(buf.at[0], buf.at[back], ssem.at[i], rsem.at[back], qdev(i))
        send(buf.at[0], buf.at[1], ssem.at[1], rsem.at[1], partner)

    spread(qq, q_s, q_r)
    loads[2].wait()
    loads[3].wait()
    gmb[...] = (g_ref[...].astype(F32) * live_col).astype(BF)
    dd[0] = nt(wall[mp].reshape(DH, D), gmb[...]).astype(BF)
    spread(dd, d_s, d_r)
    if YL == 2:
        send_row(wall, (mp, core), (mp, core), w_s, 0, w_r.at[0], (seq, head_at(1, 0)))
    prepare_keys(0)
    prepare_queries(0)
    for i in range(NQ):
        qS[i, DH : 2 * DH, :] = jnp.zeros((DH, T), BF)
        wq[i, DH : 2 * DH, :] = jnp.zeros((DH, T), BF)

    for i in range(NQ):
        m[i] = jnp.full((8, T), -1e30, F32)
        oacc[i] = jnp.zeros((2 * DH + 16, T), F32)
        dqacc[i] = jnp.zeros((DH, T), F32)

    def relay(buf, lsem, rsem, k):
        i = 2 * k
        arrive(buf.at[i], rsem.at[i])
        send_row(buf, i, i + 1, lsem, i, rsem.at[i + 1], partner)

    def forward_keys(j, hf):
        arrive(kvb.at[j, pl.ds(*CUTS[hf])], kv_r.at[2 * j + hf])
        k = (j + 1) // 2
        odd = j % 2 == 1
        if j < NZ - 1 and (k + 1 < NZ // 2 or hf == (1 if odd else 0)):
            to = j + 2 if k + 1 < NZ // 2 else NZ - 1
            send_keys(j, hf, to, kv_s, 2 * j + hf, zdev(-1 if odd else 1))

    def before(it):
        def take(js):
            for hf in range(2):
                for j in js:
                    forward_keys(j, hf)

        js = []
        if it == 0 and H > 1:
            js = [1, 2]
        if it > 1 and it + 1 < H:
            js = [2 * it + 1, 2 * it + 2]
        if it == NB - 1:
            js = [NB - 1]
        take(js)
        if it == 0:
            for k in range(1, max(NY - 1, 1)):
                relay(qq, ql_s, q_r, k)
        for half in range(2):
            if it == half * (H // 2):
                if half == 1 and it == 0:
                    relay(qq, ql_s, q_r, NY - 1)
                for i in range(half * U, half * U + U):
                    if i % 2 == 1:
                        arrive(qq.at[i], q_r.at[i])
                    if i > 0:
                        prepare_queries(i)
        if it == 0 and H > 2:
            take([3, 4])
            js = js + [3, 4]
        if it == 0 and H // 2 > 0:
            relay(qq, ql_s, q_r, NY - 1)
        for j in js:
            prepare_keys(j)
        if it == max(NB - 5, 0):
            if YL == 2:
                arrive(wall.at[0, 0], w_r.at[0])
            for dx in range(1, X):
                for flip in range(YL):
                    k = 1 + 2 * (dx - 1) + flip
                    h = head_at(flip, 0)
                    send_row(wall, (h, core), (h, core), w_s, k, w_r.at[k], (seq, head_at(0, dx)))
        if it == max(NB - 2, 0):
            for k in range(1, NY):
                relay(dd, dl_s, d_r, k)

    def step_of(n):
        late = n - 2 * H
        if isinstance(n, int):
            j = n if n < H else (n - H if late < 0 else H + late // 2)
            return j, U * (0 if n < H else (1 if late < 0 else late % 2))
        j = jnp.where(n < H, n, jnp.where(late < 0, n - H, H + jnp.right_shift(late, 1)))
        half = jnp.where(n < H, 0, jnp.where(late < 0, 1, late & 1))
        return j, half * U

    def S(n, buf):
        j, i0 = step_of(n)
        for t in range(U):
            buf[t] = nn(kvb[j, 0:T, :], qS[i0 + t])

    def E(n, buf, par):
        j, i0 = step_of(n)
        for t in range(U):
            i = i0 + t
            m_old = m[i, 0:1, :]
            m_new = jnp.maximum(m_old, jnp.max(buf[t], axis=0, keepdims=True))
            mh[j, i, 0:1, :] = m_new
            m[i, 0:1, :] = m_new
            ab[par, t, 0:1, :] = jnp.exp(m_old - m_new)
            p[j, i] = jnp.exp(buf[t] - m_new).astype(BF)

    def O(n, par):
        j, i0 = step_of(n)
        for t in range(U):
            i = i0 + t
            oacc[i] = oacc[i] * ab[par, t, 0:1, :] + nn(kvT[j], p[j, i])

    before(0)
    first, last = 0, 2 * NB - 1
    S(first, sA)
    E(first, sA, 0)
    S(first + 1, sB)

    @pl.loop(1, NB)
    def _(it):
        for fixed in range(1, NB):
            if fixed in WAITS(NB, H):
                pl.when(it == fixed)(functools.partial(before, fixed))
        n = 2 * it
        S(n, sA)
        E(n - 1, sB, 1)
        O(n - 2, 0)
        S(n + 1, sB)
        E(n, sA, 0)
        O(n - 1, 1)

    E(last, sB, 1)
    O(last - 1, 0)
    O(last, 1)
    for k in range(NY):
        arrive(dd.at[2 * k + 1], d_r.at[2 * k + 1])

    for i in range(NQ):
        total = oacc[i, 2 * DH : 2 * DH + 1, :]
        inv = 1.0 / total
        o = oacc[i, DH : 2 * DH, :] * inv
        oacc[i, 0:DH, :] = oacc[i, 0:DH, :] * inv
        osend[i % 2, i // 2] = o.astype(BF)
        lrow = m[i, 0:1, :] + jnp.log(total)
        drow = jnp.sum(o * dd[i].astype(F32), axis=0, keepdims=True)
        Ll[i, 0:1, :] = lrow
        Dl[i, 0:1, :] = drow
        stl[pl.ds(qabs(i), 1), :] = lrow
        stl[pl.ds(NQ + qabs(i), 1), :] = drow

    send(stl, pst, st_s.at[NY], st_r.at[NY], partner)
    send(osend.at[1], opair, o_s.at[NY], o_r.at[NY], partner)

    def chip_totals():
        arrive(pst, st_r.at[NY])
        la, lb = stl[0:NQ, :], pst[0:NQ, :]
        top = jnp.maximum(la, lb)
        wa, wb = jnp.exp(la - top), jnp.exp(lb - top)
        both = wa + wb
        inv = 1.0 / both
        str_[0, 0:NQ, :] = top + jnp.log(both)
        str_[0, NQ : 2 * NQ, :] = (wa * stl[NQ : 2 * NQ, :] + wb * pst[NQ : 2 * NQ, :]) * inv
        for k in range(1, NY):
            back = qback(2 * k) // 2
            send(str_.at[0], str_.at[back], st_s.at[k], st_r.at[back], qdev(2 * k))
        wpair[0] = wa * inv
        wpair[1] = wb * inv
        arrive(opair, o_r.at[NY])
        for k in range(NY):
            row = pl.ds(qabs(2 * k), 1)
            mine = osend[0, k].astype(F32) * wpair[0, row, :]
            osend[0, k] = (mine + opair[k].astype(F32) * wpair[1, row, :]).astype(BF)
        for k in range(1, NY):
            back = qback(2 * k) // 2
            send(osend.at[0, k], orecv.at[back], o_s.at[k], o_r.at[back], qdev(2 * k))

    def Ust(j, half, buf):
        for t in range(U):
            i = half * U + t
            c = jnp.exp(mh[j, i, 0:1, :] - Ll[i, 0:1, :])
            rhs = jnp.concatenate([jnp.zeros((DH, T), BF), (dd[i].astype(F32) * c).astype(BF)], axis=0)
            buf[t] = nn(kvb[j, 0:T, :], rhs) - c * Dl[i, 0:1, :]

    def Dst(j, half, buf):
        for t in range(U):
            i = half * U + t
            ds[j, i] = (p[j, i].astype(F32) * buf[t]).astype(BF)

    def Mst(j, half):
        for t in range(U):
            i = half * U + t
            dqacc[i] += nn(kvT[j, 0:DH, :], ds[j, i])

    Ust(0, 0, sA)
    Dst(0, 0, sA)
    Ust(0, 1, sB)

    def local_turn(j):
        Ust(j, 0, sA)
        Dst(j - 1, 1, sB)
        Mst(j - 1, 0)
        Ust(j, 1, sB)
        Dst(j, 0, sA)
        Mst(j - 1, 1)

    cut = min(NB, 2)
    pl.loop(1, cut)(local_turn)
    chip_totals()
    pl.loop(cut, NB)(local_turn)
    Dst(NB - 1, 1, sB)
    Mst(NB - 1, 0)
    Mst(NB - 1, 1)

    for k in range(1, NY):
        arrive(str_.at[k], st_r.at[k])
    if YL == 2:
        send_row(wall, (head_at(1, 0), core), (head_at(1, 0), core), wl_s, 0, wl_r.at[0], partner)
    for dx in range(1, X):
        for flip in range(YL):
            k = 1 + 2 * (dx - 1) + flip
            h = head_at(flip, -dx)
            arrive(wall.at[0, 0], w_r.at[k])
            send_row(wall, (h, core), (h, core), wl_s, k, wl_r.at[k], partner)
    big = str_[0, 0:NQ, :]
    for k in range(1, NY):
        big = jnp.maximum(big, str_[k, 0:NQ, :])
    wsum = jnp.zeros((NQ, T), F32)
    dsum = jnp.zeros((NQ, T), F32)
    for k in range(NY):
        wt = jnp.exp(str_[k, 0:NQ, :] - big)
        wsum = wsum + wt
        dsum = dsum + wt * str_[k, NQ : 2 * NQ, :]
    Lg[0:NQ, :] = big + jnp.log(wsum)
    Dg[0:NQ, :] = dsum / wsum
    def attended_rows():
        own = pl.ds(qabs(0), 1)
        att = jnp.exp(str_[0, own, :] - Lg[own, :]) * osend[0, 0].astype(F32)
        for k in range(1, NY):
            arrive(orecv.at[k], o_r.at[k])
            att = att + jnp.exp(str_[k, own, :] - Lg[own, :]) * orecv[k].astype(F32)
        wgp = nn(att.astype(BF), gmb[...])
        for s in range(NQ):
            wg1s[s] = wgp[s * RW : (s + 1) * RW, :].astype(BF)
        for i in range(1, NQ):
            back = qback(i)
            send(wg1s.at[qabs(i)], wg1r.at[back], g1_s.at[i], g1_r.at[back], qdev(i))
        attall[mp] = (att * live_row).astype(BF)
        for r in range(1, NMP):
            send(attall.at[mp], attall.at[mp], at_s.at[r], at_r.at[r], mdev(r))

    attended_rows()
    for i in range(NQ):
        w = jnp.exp(Ll[i, 0:1, :] - Lg[pl.ds(qabs(i), 1), :])
        e = w * (Dl[i, 0:1, :] - Dg[pl.ds(qabs(i), 1), :])
        q32 = qq[i].astype(F32)
        wq[i, 0:DH, :] = (q32 * w).astype(BF)
        rr[i, 0:DH, :] = q32 * e
        rr[i, DH : 2 * DH, :] = dd[i].astype(F32) * w
        total = (dqacc[i] * w + oacc[i, 0:DH, :] * e) * SCALE
        if i == 0:
            dqacc[0] = total
        else:
            dqacc[i] = total
            if i % 2 == 1:
                dqsend[1, i // 2] = total.astype(BF)
    send(dqsend.at[1], dqpair, dq_s.at[NY], dq_r.at[NY], partner)

    def key_pair(n):
        @pl.loop(0, 2)
        def _(b):
            j = NB - 1 - 2 * n - b
            acc = None
            for i in range(NQ):
                c = jnp.exp(mh[j, i, 0:1, :] - Ll[i, 0:1, :])
                r = nt(ds[j, i], wq[i]) + nt(p[j, i], (rr[i] * c).astype(BF))
                acc = r if acc is None else acc + r
            dkp[j] = acc

    def pass_on(j, hf):
        lo, size = hf * (T // 2), T // 2
        total = dkp[j, pl.ds(lo, size), :]
        odd = j % 2 == 1
        if j < NZ - 3 or (j == NZ - 3 and hf == 0) or (j == NZ - 2 and hf == 1):
            arrive(drecv.at[j, pl.ds(lo, size)], dk_r.at[2 * j + hf])
            total = total + drecv[j, pl.ds(lo, size), :].astype(F32)
        dsend[j, pl.ds(lo, size), :] = total.astype(BF)
        if j == NZ - 1:
            onward = hf == 0
            to = max(NZ - 3, 0) if hf == 0 else max(NZ - 2, 1)
        else:
            onward = odd
            to = j - 2 if j >= 3 else (0 if j == 1 else NZ - 1)
        send(dsend.at[j, pl.ds(lo, size)], drecv.at[to, pl.ds(lo, size)], dk_s.at[2 * j + hf], dk_r.at[2 * to + hf],
             zdev(1 if onward else -1))

    def gradient_over_z():
        wg1r[0] = wg1s[qabs(0)]
        for i in range(1, NQ):
            arrive(wg1r.at[i], g1_r.at[i])
        part = wg1r[0].astype(F32)
        for i in range(1, NQ):
            part = part + wg1r[i].astype(F32)
        wg2[z] = part.astype(BF)
        for r in range(1, NZ):
            send(wg2.at[z], wg2.at[z], g2_s.at[r], g2_r.at[r], zdev(r))

    for n in range(H):
        key_pair(n)
        if n == H - 2 and n > 0:
            gradient_over_z()
        j = NB - 1 - 2 * n
        pass_on(j, 0)
        if n > 0:
            pass_on(j + 1, 1)
        pass_on(j, 1)
        if j > 1:
            pass_on(j - 1, 0)
        if n == 0:
            arrive(dqpair, dq_r.at[NY])
            dqacc[0] += dqpair[0].astype(F32)
            for k in range(1, NY):
                dqsend[0, k] = (dqacc[2 * k] + dqpair[k].astype(F32)).astype(BF)
                back = qback(2 * k) // 2
                send(dqsend.at[0, k], dqrecv.at[back], dq_s.at[k], dq_r.at[back], qdev(2 * k))
    if H <= 2:
        gradient_over_z()

    for r in range(1, NZ):
        arrive(wg2.at[0], g2_r.at[r])
    part = wg2[0].astype(F32)
    for k in range(1, NZ):
        part = part + wg2[k].astype(F32)
    own = qabs(0)
    wg3[own] = part.astype(BF)
    for i in range(1, NQ):
        send(wg3.at[own], wg3.at[own], g3_s.at[i], g3_r.at[qback(i)], qdev(i))

    for r in range(1, NMP):
        arrive(wall.at[0, 0], wl_r.at[r - 1])
        arrive(attall.at[0], at_r.at[r])
    att_rows = attall[...].reshape(NMP * DH, T).astype(F32).T.astype(BF)
    out_ref[...] = nn(att_rows, wall[...].reshape(NMP * DH, D)).astype(BF)

    total = dqacc[0]
    for k in range(1, NY):
        arrive(dqrecv.at[k], dq_r.at[k])
        total = total + dqrecv[k].astype(F32)
    dq_ref[...] = total

    for hf in range(2):
        rows_of = pl.ds(hf * (T // 2), T // 2)
        total = dkp[0, rows_of, :]
        for slot in (0, NB - 1):
            if NZ > 2 or slot == hf:
                arrive(drecv.at[slot, rows_of], dk_r.at[2 * slot + hf])
                total = total + drecv[slot, rows_of, :].astype(F32)
        dkv_ref[rows_of, :] = total * live_col[hf * (T // 2) : (hf + 1) * (T // 2), :]

    for i in range(1, NQ):
        arrive(wg3.at[0], g3_r.at[i])
    for s in range(NQ):
        wg_ref[s * RW : (s + 1) * RW, :] = wg3[s].astype(F32)

    for make in copies:
        src, ssem = make()
        rcopy(src, src, ssem, kv_r.at[0], partner).wait_send()


def WAITS(NB, H):
    return set(range(1, H - 1)) | {H // 2, NB - 1, max(NB - 5, 0), max(NB - 2, 0)}


def write_out(a_ref, b_ref, c_ref, d_ref, a_hbm, b_hbm, c_hbm, d_hbm, sem):
    pairs = ((a_ref, a_hbm), (b_ref, b_hbm), (c_ref, c_hbm), (d_ref, d_hbm))
    copies = [pltpu.make_async_copy(r, h, sem.at[n]) for n, (r, h) in enumerate(pairs)]
    for c in copies:
        c.start()
    for c in copies:
        c.wait()


def solution(mesh):
    NMP = mesh.shape["mp"]
    NSEQ = mesh.shape["seq"]
    NY, NZ = {64: (4, 8), 8: (2, 2), 16: (2, 4)}[NSEQ]
    NB, NQ = NZ, NY * CORES
    U = NQ // 2

    def shards(queries, key_value, tile_fill, out_weight, grad_output):
        T = queries.shape[0]
        D = out_weight.shape[2]
        qT = queries[:, 0, :].T
        kv = key_value[:, 0, :]
        w = out_weight.reshape(CORES, DH // CORES, out_weight.shape[2])
        V = pl.BlockSpec(memory_space=pltpu.VMEM)
        A = pl.BlockSpec(memory_space=pl.ANY)
        v = pltpu.VMEM
        dma = lambda n: pltpu.SemaphoreType.DMA((n,))
        RW = DH // NQ
        scratch = [
            pltpu.SMEM((T // TILE,), jnp.int32), v((DH, T), BF), v((T, 2 * DH), BF), v((T, D), BF), dma(5),
            v((NB, T + 16, 2 * DH), BF), v((NB, 2 * DH + 16, T), BF), v((NQ, DH, T), BF), v((NQ, DH, T), BF),
            v((NQ, 2 * DH, T), BF), v((NB, NQ, T, T), BF), v((NB, NQ, 8, T), F32), v((NQ, 8, T), F32),
            v((NQ, 2 * DH + 16, T), F32), v((2, U, 8, T), F32), v((NB, NQ, T, T), BF),
            v((U, T, T), F32), v((U, T, T), F32), v((NQ, 8, T), F32), v((NQ, 8, T), F32),
            v((NQ, 2 * DH, T), F32), v((NQ, 2 * DH, T), BF),
            v((2 * NQ, T), F32), v((2 * NQ, T), F32), v((NY, 2 * NQ, T), F32), v((2, NQ, T), F32), v((8, T), F32), v((8, T), F32),
            v((2, NY, DH, T), BF), v((NY, DH, T), BF), v((NY, DH, T), BF), v((NB, T, 2 * DH), F32), v((NB, T, 2 * DH), BF), v((NB, T, 2 * DH), BF),
            v((NQ, DH, T), F32), v((2, NY, DH, T), BF), v((NY, DH, T), BF), v((NY, DH, T), BF),
            v((T, D), BF), v((NMP, CORES, DH // CORES, D), BF), v((NMP, DH, T), BF),
            v((NQ, RW, D), BF), v((NQ, RW, D), BF), v((NZ, RW, D), BF), v((NQ, RW, D), BF),
            dma(4), dma(2 * NB), dma(2 * NB), dma(NQ), dma(NQ), dma(NQ), dma(NQ), dma(NQ), dma(NQ), dma(NQ), dma(NQ),
            dma(NQ), dma(NQ), dma(2 * NB), dma(2 * NB), dma(NQ), dma(NQ),
            dma(NMP), dma(NMP), dma(NMP), dma(NMP), dma(NMP), dma(NMP), dma(NQ), dma(NQ), dma(NZ), dma(NZ), dma(NQ), dma(NQ),
        ]
        shapes = [((T, D), BF), ((DH, T), F32), ((T, 2 * DH), F32), ((DH, D), F32)]
        results = pl.pallas_call(
            functools.partial(kernel, NY, NZ, NMP),
            name="voxel_attention",
            out_shape=[pltpu.VMEM(*s) for s in shapes],
            in_specs=[A, A, A, A, A],
            out_specs=[V, V, V, V],
            scratch_shapes=scratch,
            compiler_params=pltpu.CompilerParams(
                collective_id=0, has_side_effects=True, vmem_limit_bytes=56 * 1024 * 1024
            ),
        )(tile_fill, qT, kv, w, grad_output)
        out, dqT, dkv, wg = pl.pallas_call(
            write_out,
            name="write_out",
            out_shape=[jax.ShapeDtypeStruct(*s) for s in shapes],
            in_specs=[V, V, V, V],
            out_specs=[A, A, A, A],
            scratch_shapes=[dma(4)],
        )(*(pltpu.with_memory_space_constraint(r, pltpu.VMEM) for r in results))
        return out, dqT.T[:, None, :], dkv[:, None, :], wg[None]

    return jax.shard_map(
        shards,
        mesh=mesh,
        in_specs=(
            P("seq", "mp", None),
            P("seq", "mp", None),
            P("seq"),
            P("mp", None, None),
            P("seq", None),
        ),
        out_specs=(P("seq", None), P("seq", "mp", None), P("seq", "mp", None), P("mp", None, None)),
        check_vma=False,
    )
```

```python
import functools

import jax
import jax.numpy as jnp
from jax import lax
from jax.experimental import pallas as pl
from jax.experimental.pallas import tpu as pltpu
from jax.sharding import PartitionSpec as P

MESH = pl.DeviceIdType.MESH
BF = jnp.bfloat16
F32 = jnp.float32
TILE = 128
DH = 64
CORES = 2


def nn(a, b):
    return jnp.dot(a, b, preferred_element_type=F32)


def nt(a, b):
    return lax.dot_general(a, b, (((1,), (1,)), ((), ())), preferred_element_type=F32)


def place(offset, size):
    o = offset % size
    if o > size // 2:
        o -= size
    return 2 * o - 1 if o > 0 else -2 * o


def offset_of(rank):
    half = (rank + 1) // 2
    return half if rank % 2 == 1 else -half


def kernel(
    NY, NZ, NMP,
    fill_hbm, qT_hbm, kv_hbm, w_hbm, g_hbm,
    out_ref, dq_ref, dkv_ref, wg_ref,
    fill_ref, qT_ref, kv_ref, g_ref, in_sem,
    kvb, kvT, qq, dd, qS, p, mh, m, oacc, ab, ds,
    sA, sB, Ll, Dl, rr, wq,
    stl, pst, str_, wpair, Lg, Dg, osend, opair, orecv, dkp, dsend, drecv, dqacc, dqsend, dqpair, dqrecv,
    gmb, wall, attall, wg1s, wg1r, wg2, wg3,
    kv0_s, kv_s, kv_r, qf_s, qf_r, q_s, q_r, ql_s, d_s, d_r, dl_s, st_s, st_r, o_s, o_r, dk_s, dk_r, dq_s, dq_r,
    w_s, w_r, wl_s, wl_r, at_s, at_r, g1_s, g1_r, g2_s, g2_r, g3_s, g3_r,
):
    T = kv_ref.shape[0]
    D = wall.shape[3]
    NB, NQ = NZ, NY * CORES
    U = NQ // 2
    H = NB // 2
    RW = DH // NQ
    YL = 2 if NMP % 2 == 0 else 1
    X = NMP // YL
    CUTS = ((0, 144), (144, 128))
    SCALE = DH**-0.5

    seq = lax.axis_index("seq")
    mp = lax.axis_index("mp")
    core = seq % CORES
    z = (seq // CORES) % NZ
    y = seq // (CORES * NZ)

    def zdev(o):
        return ((y * NZ + (z + o + NZ) % NZ) * CORES + core, mp)

    def qoff(i):
        return offset_of(i // 2) % NY, i % 2

    def qdev(i):
        dy, dc = qoff(i)
        return ((((y + dy) % NY) * NZ + z) * CORES + (core + dc) % 2, mp)

    def qabs(i):
        dy, dc = qoff(i)
        return ((y + dy) % NY) * CORES + (core + dc) % 2

    def qback(i):
        dy, dc = qoff(i)
        return 2 * place(-dy, NY) + dc

    def mdev(r):
        return (seq, (mp + r) % NMP)

    def head_at(flip, dx):
        return ((mp // X + flip) % YL) * X + (mp % X + dx + X) % X

    partner = qdev(1)

    def rcopy(src, dst, ssem, rsem, dev):
        return pltpu.make_async_remote_copy(
            src_ref=src, dst_ref=dst, send_sem=ssem, recv_sem=rsem, device_id=dev, device_id_type=MESH
        )

    barrier = pltpu.get_barrier_semaphore()
    near = [zdev(offset_of(j)) for j in range(1, min(NB, 3))] + [partner]
    near += [qdev(2 * k) for k in range(1, min(NY, 3))]
    near += [(seq, head_at(1, 0))] * (YL - 1) + [(seq, head_at(0, dx)) for dx in range(1, X)]
    for dev in near:
        pl.semaphore_signal(barrier, inc=1, device_id=dev, device_id_type=MESH)

    w_ref = wall.at[mp]
    loads = [
        pltpu.make_async_copy(a, b, in_sem.at[n])
        for n, (a, b) in enumerate(((kv_hbm, kv_ref), (qT_hbm, qT_ref), (w_hbm, w_ref), (g_hbm, g_ref), (fill_hbm, fill_ref)))
    ]
    for c in loads:
        c.start()

    rows = lax.broadcasted_iota(jnp.int32, (T, 1), 0)
    loads[4].wait()
    fills = [fill_ref[t] for t in range(T // TILE)]
    live_col = jnp.zeros((T, 1), F32)
    for t in range(T // TILE):
        inside = (rows >= t * TILE) & (rows < t * TILE + fills[t])
        live_col = jnp.where(inside, 1.0, live_col)
    lanes = lax.broadcasted_iota(jnp.int32, (1, T), 1)
    live_row = jnp.zeros((1, T), F32)
    for t in range(T // TILE):
        inside = (lanes >= t * TILE) & (lanes < t * TILE + fills[t])
        live_row = jnp.where(inside, 1.0, live_row)
    loads[0].wait()
    kv = kv_ref[...].astype(F32)
    is_key = lax.broadcasted_iota(jnp.int32, (1, 2 * DH), 1) < DH
    stand_in = jnp.where(is_key, kv[0:1, :], 0.0)
    kvb[0, 0:T, :] = jnp.where(live_col > 0.0, kv, stand_in).astype(BF)
    tail_rows = lax.broadcasted_iota(jnp.int32, (16, 1), 0)
    tail = jnp.zeros((16, TILE), F32)
    for t in range(T // TILE):
        tail = jnp.where(tail_rows == t, live_row[:, t * TILE : (t + 1) * TILE], tail)
    kvb[0, T : T + 16, :] = tail.astype(BF)
    loads[1].wait()
    qq[0] = (qT_ref[...].astype(F32) * SCALE).astype(BF)

    def prepare_keys(j):
        live16 = kvb[j, T : T + 16, :].astype(F32)
        row = jnp.concatenate([live16[t : t + 1, :] for t in range(T // TILE)], axis=1)
        kvT[j, 0 : 2 * DH, :] = (kvb[j, 0:T, :].astype(F32).T * row).astype(BF)
        kvT[j, 2 * DH : 2 * DH + 16, :] = jnp.broadcast_to(row, (16, T)).astype(BF)

    def prepare_queries(i):
        qS[i, 0:DH, :] = qq[i]

    pl.semaphore_wait(barrier, len(near))

    copies = []

    def send(src, dst, ssem, rsem, dev):
        rcopy(src, dst, ssem, rsem, dev).start()
        copies.append(lambda: (src, ssem))

    def send_row(buf, a, b, ssem, k, rsem, dev):
        rcopy(buf.at[a], buf.at[b], ssem.at[k], rsem, dev).start()
        copies.append(lambda: (buf.at[(0, 0) if isinstance(a, tuple) else 0], ssem.at[k]))

    def arrive(dst, rsem):
        rcopy(dst, dst, kv0_s.at[0], rsem, partner).wait_recv()

    def send_keys(j, hf, to, sem, k, dev):
        lo, size = CUTS[hf]
        src, dst = kvb.at[j, pl.ds(lo, size)], kvb.at[to, pl.ds(lo, size)]
        rcopy(src, dst, sem.at[k], kv_r.at[2 * to + hf], dev).start()
        copies.append(lambda: (kvb.at[0, pl.ds(lo, size)], sem.at[k]))

    right = place(-1, NZ)
    for hf in range(2):
        if NZ > 2 or hf == 0:
            send_keys(0, hf, right, kv0_s, hf, zdev(1))
        if NZ > 2 or hf == 1:
            send_keys(0, hf, 1, kv0_s, 2 + hf, zdev(-1))

    def spread(buf, ssem, rsem):
        for k in range(1, min(NY, 3)):
            i, back = 2 * k, qback(2 * k)
            send(buf.at[0], buf.at[back], ssem.at[i], rsem.at[back], qdev(i))
        send(buf.at[0], buf.at[1], ssem.at[1], rsem.at[1], partner)

    spread(qq, q_s, q_r)
    loads[2].wait()
    loads[3].wait()
    gmb[...] = (g_ref[...].astype(F32) * live_col).astype(BF)
    dd[0] = nt(wall[mp].reshape(DH, D), gmb[...]).astype(BF)
    spread(dd, d_s, d_r)
    if YL == 2:
        send_row(wall, (mp, core), (mp, core), w_s, 0, w_r.at[0], (seq, head_at(1, 0)))
    prepare_keys(0)
    prepare_queries(0)
    for i in range(NQ):
        qS[i, DH : 2 * DH, :] = jnp.zeros((DH, T), BF)
        wq[i, DH : 2 * DH, :] = jnp.zeros((DH, T), BF)

    for i in range(NQ):
        m[i] = jnp.full((8, T), -1e30, F32)
        oacc[i] = jnp.zeros((2 * DH + 16, T), F32)
        dqacc[i] = jnp.zeros((DH, T), F32)

    def relay(buf, lsem, rsem, k):
        i = 2 * k
        arrive(buf.at[i], rsem.at[i])
        send_row(buf, i, i + 1, lsem, i, rsem.at[i + 1], partner)

    def forward_keys(j, hf):
        arrive(kvb.at[j, pl.ds(*CUTS[hf])], kv_r.at[2 * j + hf])
        k = (j + 1) // 2
        odd = j % 2 == 1
        if j < NZ - 1 and (k + 1 < NZ // 2 or hf == (1 if odd else 0)):
            to = j + 2 if k + 1 < NZ // 2 else NZ - 1
            send_keys(j, hf, to, kv_s, 2 * j + hf, zdev(-1 if odd else 1))

    def before(it):
        def take(js):
            for hf in range(2):
                for j in js:
                    forward_keys(j, hf)

        js = []
        if it == 0 and H > 1:
            js = [1, 2]
        if it > 1 and it + 1 < H:
            js = [2 * it + 1, 2 * it + 2]
        if it == NB - 1:
            js = [NB - 1]
        take(js)
        if it == 0:
            for k in range(1, min(NY, 3)):
                relay(qq, ql_s, q_r, k)
                if NY == 4:
                    cut = pl.ds((k - 1) * (DH // 2), DH // 2)
                    send(qq.at[2 * k, cut], qq.at[6, cut], qf_s.at[k - 1], qf_r.at[k - 1], qdev(6 - 2 * k))
            if H > 2:
                take([3, 4])
                js = js + [3, 4]
            if NY == 4:
                for k in range(1, 3):
                    arrive(qq.at[6, pl.ds((k - 1) * (DH // 2), DH // 2)], qf_r.at[k - 1])
                send(qq.at[6], qq.at[7], ql_s.at[6], q_r.at[7], partner)
                send(dd.at[0], dd.at[6], d_s.at[6], d_r.at[6], qdev(6))
        for half in range(2):
            if it == half * (H // 2):
                for i in range(half * U, half * U + U):
                    if i % 2 == 1:
                        arrive(qq.at[i], q_r.at[i])
                    if i > 0:
                        prepare_queries(i)
        for j in js:
            prepare_keys(j)
        if it == max(NB - 5, 0):
            if YL == 2:
                arrive(wall.at[0, 0], w_r.at[0])
            for dx in range(1, X):
                for flip in range(YL):
                    k = 1 + 2 * (dx - 1) + flip
                    h = head_at(flip, 0)
                    send_row(wall, (h, core), (h, core), w_s, k, w_r.at[k], (seq, head_at(0, dx)))
        if it == max(NB - 2, 0):
            for k in range(1, NY):
                relay(dd, dl_s, d_r, k)

    def step_of(n):
        late = n - 2 * H
        if isinstance(n, int):
            j = n if n < H else (n - H if late < 0 else H + late // 2)
            return j, U * (0 if n < H else (1 if late < 0 else late % 2))
        j = jnp.where(n < H, n, jnp.where(late < 0, n - H, H + jnp.right_shift(late, 1)))
        half = jnp.where(n < H, 0, jnp.where(late < 0, 1, late & 1))
        return j, half * U

    def S(n, buf):
        j, i0 = step_of(n)
        for t in range(U):
            buf[t] = nn(kvb[j, 0:T, :], qS[i0 + t])

    def E(n, buf, par):
        j, i0 = step_of(n)
        for t in range(U):
            i = i0 + t
            m_old = m[i, 0:1, :]
            m_new = jnp.maximum(m_old, jnp.max(buf[t], axis=0, keepdims=True))
            mh[j, i, 0:1, :] = m_new
            m[i, 0:1, :] = m_new
            ab[par, t, 0:1, :] = jnp.exp(m_old - m_new)
            p[j, i] = jnp.exp(buf[t] - m_new).astype(BF)

    def O(n, par):
        j, i0 = step_of(n)
        for t in range(U):
            i = i0 + t
            oacc[i] = oacc[i] * ab[par, t, 0:1, :] + nn(kvT[j], p[j, i])

    before(0)
    first, last = 0, 2 * NB - 1
    S(first, sA)
    E(first, sA, 0)
    S(first + 1, sB)

    @pl.loop(1, NB)
    def _(it):
        for fixed in range(1, NB):
            if fixed in WAITS(NB, H):
                pl.when(it == fixed)(functools.partial(before, fixed))
        n = 2 * it
        S(n, sA)
        E(n - 1, sB, 1)
        O(n - 2, 0)
        S(n + 1, sB)
        E(n, sA, 0)
        O(n - 1, 1)

    E(last, sB, 1)
    O(last - 1, 0)
    O(last, 1)
    for k in range(NY):
        arrive(dd.at[2 * k + 1], d_r.at[2 * k + 1])

    for i in range(NQ):
        total = oacc[i, 2 * DH : 2 * DH + 1, :]
        inv = 1.0 / total
        o = oacc[i, DH : 2 * DH, :] * inv
        oacc[i, 0:DH, :] = oacc[i, 0:DH, :] * inv
        osend[i % 2, i // 2] = o.astype(BF)
        lrow = m[i, 0:1, :] + jnp.log(total)
        drow = jnp.sum(o * dd[i].astype(F32), axis=0, keepdims=True)
        Ll[i, 0:1, :] = lrow
        Dl[i, 0:1, :] = drow
        stl[pl.ds(qabs(i), 1), :] = lrow
        stl[pl.ds(NQ + qabs(i), 1), :] = drow

    send(stl, pst, st_s.at[NY], st_r.at[NY], partner)
    send(osend.at[1], opair, o_s.at[NY], o_r.at[NY], partner)

    def chip_totals():
        arrive(pst, st_r.at[NY])
        la, lb = stl[0:NQ, :], pst[0:NQ, :]
        top = jnp.maximum(la, lb)
        wa, wb = jnp.exp(la - top), jnp.exp(lb - top)
        both = wa + wb
        inv = 1.0 / both
        str_[0, 0:NQ, :] = top + jnp.log(both)
        str_[0, NQ : 2 * NQ, :] = (wa * stl[NQ : 2 * NQ, :] + wb * pst[NQ : 2 * NQ, :]) * inv
        for k in range(1, NY):
            back = qback(2 * k) // 2
            send(str_.at[0], str_.at[back], st_s.at[k], st_r.at[back], qdev(2 * k))
        wpair[0] = wa * inv
        wpair[1] = wb * inv
        arrive(opair, o_r.at[NY])
        for k in range(NY):
            row = pl.ds(qabs(2 * k), 1)
            mine = osend[0, k].astype(F32) * wpair[0, row, :]
            osend[0, k] = (mine + opair[k].astype(F32) * wpair[1, row, :]).astype(BF)
        for k in range(1, NY):
            back = qback(2 * k) // 2
            send(osend.at[0, k], orecv.at[back], o_s.at[k], o_r.at[back], qdev(2 * k))

    def Ust(j, half, buf):
        for t in range(U):
            i = half * U + t
            c = jnp.exp(mh[j, i, 0:1, :] - Ll[i, 0:1, :])
            rhs = jnp.concatenate([jnp.zeros((DH, T), BF), (dd[i].astype(F32) * c).astype(BF)], axis=0)
            buf[t] = nn(kvb[j, 0:T, :], rhs) - c * Dl[i, 0:1, :]

    def Dst(j, half, buf):
        for t in range(U):
            i = half * U + t
            ds[j, i] = (p[j, i].astype(F32) * buf[t]).astype(BF)

    def Mst(j, half):
        for t in range(U):
            i = half * U + t
            dqacc[i] += nn(kvT[j, 0:DH, :], ds[j, i])

    Ust(0, 0, sA)
    Dst(0, 0, sA)
    Ust(0, 1, sB)

    def local_turn(j):
        Ust(j, 0, sA)
        Dst(j - 1, 1, sB)
        Mst(j - 1, 0)
        Ust(j, 1, sB)
        Dst(j, 0, sA)
        Mst(j - 1, 1)

    cut = min(NB, 2)
    pl.loop(1, cut)(local_turn)
    chip_totals()
    pl.loop(cut, NB)(local_turn)
    Dst(NB - 1, 1, sB)
    Mst(NB - 1, 0)
    Mst(NB - 1, 1)

    for k in range(1, NY):
        arrive(str_.at[k], st_r.at[k])
    if YL == 2:
        send_row(wall, (head_at(1, 0), core), (head_at(1, 0), core), wl_s, 0, wl_r.at[0], partner)
    for dx in range(1, X):
        for flip in range(YL):
            k = 1 + 2 * (dx - 1) + flip
            h = head_at(flip, -dx)
            arrive(wall.at[0, 0], w_r.at[k])
            send_row(wall, (h, core), (h, core), wl_s, k, wl_r.at[k], partner)
    big = str_[0, 0:NQ, :]
    for k in range(1, NY):
        big = jnp.maximum(big, str_[k, 0:NQ, :])
    wsum = jnp.zeros((NQ, T), F32)
    dsum = jnp.zeros((NQ, T), F32)
    for k in range(NY):
        wt = jnp.exp(str_[k, 0:NQ, :] - big)
        wsum = wsum + wt
        dsum = dsum + wt * str_[k, NQ : 2 * NQ, :]
    Lg[0:NQ, :] = big + jnp.log(wsum)
    Dg[0:NQ, :] = dsum / wsum
    def attended_rows():
        own = pl.ds(qabs(0), 1)
        att = jnp.exp(str_[0, own, :] - Lg[own, :]) * osend[0, 0].astype(F32)
        for k in range(1, NY):
            arrive(orecv.at[k], o_r.at[k])
            att = att + jnp.exp(str_[k, own, :] - Lg[own, :]) * orecv[k].astype(F32)
        wgp = nn(att.astype(BF), gmb[...])
        for s in range(NQ):
            wg1s[s] = wgp[s * RW : (s + 1) * RW, :].astype(BF)
        for i in range(1, NQ):
            back = qback(i)
            send(wg1s.at[qabs(i)], wg1r.at[back], g1_s.at[i], g1_r.at[back], qdev(i))
        attall[mp] = (att * live_row).astype(BF)
        for r in range(1, NMP):
            send(attall.at[mp], attall.at[mp], at_s.at[r], at_r.at[r], mdev(r))

    for i in range(NQ):
        w = jnp.exp(Ll[i, 0:1, :] - Lg[pl.ds(qabs(i), 1), :])
        e = w * (Dl[i, 0:1, :] - Dg[pl.ds(qabs(i), 1), :])
        q32 = qq[i].astype(F32)
        wq[i, 0:DH, :] = (q32 * w).astype(BF)
        rr[i, 0:DH, :] = q32 * e
        rr[i, DH : 2 * DH, :] = dd[i].astype(F32) * w
        total = (dqacc[i] * w + oacc[i, 0:DH, :] * e) * SCALE
        if i == 0:
            dqacc[0] = total
        else:
            dqacc[i] = total
            if i % 2 == 1:
                dqsend[1, i // 2] = total.astype(BF)
    send(dqsend.at[1], dqpair, dq_s.at[NY], dq_r.at[NY], partner)

    def key_pair(n):
        @pl.loop(0, 2)
        def _(b):
            j = NB - 1 - 2 * n - b
            acc = None
            for i in range(NQ):
                c = jnp.exp(mh[j, i, 0:1, :] - Ll[i, 0:1, :])
                r = nt(ds[j, i], wq[i]) + nt(p[j, i], (rr[i] * c).astype(BF))
                acc = r if acc is None else acc + r
            dkp[j] = acc

    def pass_on(j, hf):
        lo, size = hf * (T // 2), T // 2
        total = dkp[j, pl.ds(lo, size), :]
        odd = j % 2 == 1
        if j < NZ - 3 or (j == NZ - 3 and hf == 0) or (j == NZ - 2 and hf == 1):
            arrive(drecv.at[j, pl.ds(lo, size)], dk_r.at[2 * j + hf])
            total = total + drecv[j, pl.ds(lo, size), :].astype(F32)
        dsend[j, pl.ds(lo, size), :] = total.astype(BF)
        if j == NZ - 1:
            onward = hf == 0
            to = max(NZ - 3, 0) if hf == 0 else max(NZ - 2, 1)
        else:
            onward = odd
            to = j - 2 if j >= 3 else (0 if j == 1 else NZ - 1)
        send(dsend.at[j, pl.ds(lo, size)], drecv.at[to, pl.ds(lo, size)], dk_s.at[2 * j + hf], dk_r.at[2 * to + hf],
             zdev(1 if onward else -1))

    def gradient_over_z():
        wg1r[0] = wg1s[qabs(0)]
        for i in range(1, NQ):
            arrive(wg1r.at[i], g1_r.at[i])
        part = wg1r[0].astype(F32)
        for i in range(1, NQ):
            part = part + wg1r[i].astype(F32)
        wg2[z] = part.astype(BF)
        for r in range(1, NZ):
            send(wg2.at[z], wg2.at[z], g2_s.at[r], g2_r.at[r], zdev(r))

    for n in range(H):
        key_pair(n)
        j = NB - 1 - 2 * n
        pass_on(j, 0)
        if n > 0:
            pass_on(j + 1, 1)
        pass_on(j, 1)
        if j > 1:
            pass_on(j - 1, 0)
        if n == H - 2 and n > 0:
            gradient_over_z()
        if n == 0:
            attended_rows()
            arrive(dqpair, dq_r.at[NY])
            dqacc[0] += dqpair[0].astype(F32)
            for k in range(1, NY):
                dqsend[0, k] = (dqacc[2 * k] + dqpair[k].astype(F32)).astype(BF)
                back = qback(2 * k) // 2
                send(dqsend.at[0, k], dqrecv.at[back], dq_s.at[k], dq_r.at[back], qdev(2 * k))
    if H <= 2:
        gradient_over_z()

    for r in range(1, NMP):
        arrive(wall.at[0, 0], wl_r.at[r - 1])
        arrive(attall.at[0], at_r.at[r])
    att_rows = attall[...].reshape(NMP * DH, T).astype(F32).T.astype(BF)
    out_ref[...] = nn(att_rows, wall[...].reshape(NMP * DH, D)).astype(BF)

    for r in range(1, NZ):
        arrive(wg2.at[0], g2_r.at[r])
    part = wg2[0].astype(F32)
    for k in range(1, NZ):
        part = part + wg2[k].astype(F32)
    own = qabs(0)
    wg3[own] = part.astype(BF)
    for i in range(1, NQ):
        send(wg3.at[own], wg3.at[own], g3_s.at[i], g3_r.at[qback(i)], qdev(i))

    total = dqacc[0]
    for k in range(1, NY):
        arrive(dqrecv.at[k], dq_r.at[k])
        total = total + dqrecv[k].astype(F32)
    dq_ref[...] = total

    for hf in range(2):
        rows_of = pl.ds(hf * (T // 2), T // 2)
        total = dkp[0, rows_of, :]
        for slot in (0, NB - 1):
            if NZ > 2 or slot == hf:
                arrive(drecv.at[slot, rows_of], dk_r.at[2 * slot + hf])
                total = total + drecv[slot, rows_of, :].astype(F32)
        dkv_ref[rows_of, :] = total * live_col[hf * (T // 2) : (hf + 1) * (T // 2), :]

    for i in range(1, NQ):
        arrive(wg3.at[0], g3_r.at[i])
    for s in range(NQ):
        wg_ref[s * RW : (s + 1) * RW, :] = wg3[s].astype(F32)

    for make in copies:
        src, ssem = make()
        rcopy(src, src, ssem, kv_r.at[0], partner).wait_send()


def WAITS(NB, H):
    return set(range(1, H - 1)) | {H // 2, NB - 1, max(NB - 5, 0), max(NB - 2, 0)}


def write_out(a_ref, b_ref, c_ref, d_ref, a_hbm, b_hbm, c_hbm, d_hbm, sem):
    pairs = ((a_ref, a_hbm), (b_ref, b_hbm), (c_ref, c_hbm), (d_ref, d_hbm))
    copies = [pltpu.make_async_copy(r, h, sem.at[n]) for n, (r, h) in enumerate(pairs)]
    for c in copies:
        c.start()
    for c in copies:
        c.wait()


def solution(mesh):
    NMP = mesh.shape["mp"]
    NSEQ = mesh.shape["seq"]
    NY, NZ = {64: (4, 8), 8: (2, 2), 16: (2, 4)}[NSEQ]
    NB, NQ = NZ, NY * CORES
    U = NQ // 2

    def shards(queries, key_value, tile_fill, out_weight, grad_output):
        T = queries.shape[0]
        D = out_weight.shape[2]
        qT = queries[:, 0, :].T
        kv = key_value[:, 0, :]
        w = out_weight.reshape(CORES, DH // CORES, out_weight.shape[2])
        V = pl.BlockSpec(memory_space=pltpu.VMEM)
        A = pl.BlockSpec(memory_space=pl.ANY)
        v = pltpu.VMEM
        dma = lambda n: pltpu.SemaphoreType.DMA((n,))
        RW = DH // NQ
        scratch = [
            pltpu.SMEM((T // TILE,), jnp.int32), v((DH, T), BF), v((T, 2 * DH), BF), v((T, D), BF), dma(5),
            v((NB, T + 16, 2 * DH), BF), v((NB, 2 * DH + 16, T), BF), v((NQ, DH, T), BF), v((NQ, DH, T), BF),
            v((NQ, 2 * DH, T), BF), v((NB, NQ, T, T), BF), v((NB, NQ, 8, T), F32), v((NQ, 8, T), F32),
            v((NQ, 2 * DH + 16, T), F32), v((2, U, 8, T), F32), v((NB, NQ, T, T), BF),
            v((U, T, T), F32), v((U, T, T), F32), v((NQ, 8, T), F32), v((NQ, 8, T), F32),
            v((NQ, 2 * DH, T), F32), v((NQ, 2 * DH, T), BF),
            v((2 * NQ, T), F32), v((2 * NQ, T), F32), v((NY, 2 * NQ, T), F32), v((2, NQ, T), F32), v((8, T), F32), v((8, T), F32),
            v((2, NY, DH, T), BF), v((NY, DH, T), BF), v((NY, DH, T), BF), v((NB, T, 2 * DH), F32), v((NB, T, 2 * DH), BF), v((NB, T, 2 * DH), BF),
            v((NQ, DH, T), F32), v((2, NY, DH, T), BF), v((NY, DH, T), BF), v((NY, DH, T), BF),
            v((T, D), BF), v((NMP, CORES, DH // CORES, D), BF), v((NMP, DH, T), BF),
            v((NQ, RW, D), BF), v((NQ, RW, D), BF), v((NZ, RW, D), BF), v((NQ, RW, D), BF),
            dma(4), dma(2 * NB), dma(2 * NB), dma(2), dma(2), dma(NQ), dma(NQ), dma(NQ), dma(NQ), dma(NQ), dma(NQ), dma(NQ), dma(NQ),
            dma(NQ), dma(NQ), dma(2 * NB), dma(2 * NB), dma(NQ), dma(NQ),
            dma(NMP), dma(NMP), dma(NMP), dma(NMP), dma(NMP), dma(NMP), dma(NQ), dma(NQ), dma(NZ), dma(NZ), dma(NQ), dma(NQ),
        ]
        shapes = [((T, D), BF), ((DH, T), F32), ((T, 2 * DH), F32), ((DH, D), F32)]
        results = pl.pallas_call(
            functools.partial(kernel, NY, NZ, NMP),
            name="voxel_attention",
            out_shape=[pltpu.VMEM(*s) for s in shapes],
            in_specs=[A, A, A, A, A],
            out_specs=[V, V, V, V],
            scratch_shapes=scratch,
            compiler_params=pltpu.CompilerParams(
                collective_id=0, has_side_effects=True, vmem_limit_bytes=56 * 1024 * 1024
            ),
        )(tile_fill, qT, kv, w, grad_output)
        out, dqT, dkv, wg = pl.pallas_call(
            write_out,
            name="write_out",
            out_shape=[jax.ShapeDtypeStruct(*s) for s in shapes],
            in_specs=[V, V, V, V],
            out_specs=[A, A, A, A],
            scratch_shapes=[dma(4)],
        )(*(pltpu.with_memory_space_constraint(r, pltpu.VMEM) for r in results))
        return out, dqT.T[:, None, :], dkv[:, None, :], wg[None]

    return jax.shard_map(
        shards,
        mesh=mesh,
        in_specs=(
            P("seq", "mp", None),
            P("seq", "mp", None),
            P("seq"),
            P("mp", None, None),
            P("seq", None),
        ),
        out_specs=(P("seq", None), P("seq", "mp", None), P("seq", "mp", None), P("mp", None, None)),
        check_vma=False,
    )
```

```python
import functools

import jax
import jax.numpy as jnp
from jax import lax
from jax.experimental import pallas as pl
from jax.experimental.pallas import tpu as pltpu
from jax.sharding import PartitionSpec as P

MESH = pl.DeviceIdType.MESH
BF = jnp.bfloat16
F32 = jnp.float32
TILE = 128
DH = 64
CORES = 2


def nn(a, b):
    return jnp.dot(a, b, preferred_element_type=F32)


def nt(a, b):
    return lax.dot_general(a, b, (((1,), (1,)), ((), ())), preferred_element_type=F32)


def place(offset, size):
    o = offset % size
    if o > size // 2:
        o -= size
    return 2 * o - 1 if o > 0 else -2 * o


def offset_of(rank):
    half = (rank + 1) // 2
    return half if rank % 2 == 1 else -half


def kernel(
    NY, NZ, NMP,
    fill_hbm, qT_hbm, kv_hbm, w_hbm, g_hbm,
    out_ref, dq_ref, dkv_ref, wg_ref,
    fill_ref, qT_ref, kv_ref, g_ref, in_sem,
    kvb, kvT, qq, dd, qS, p, mh, m, oacc, ab, ds,
    sA, sB, Ll, Dl, rr, wq,
    stl, pst, str_, wpair, Lg, Dg, osend, opair, orecv, dkp, dsend, drecv, dqacc, dqsend, dqpair, dqrecv,
    gmb, wall, attall, wg1s, wg1r, wg2, wg3,
    kv0_s, kv_s, kv_r, qf_s, qf_r, df_s, df_r, q_s, q_r, ql_s, d_s, d_r, dl_s, st_s, st_r, o_s, o_r, dk_s, dk_r, dq_s, dq_r,
    w_s, w_r, wl_s, wl_r, at_s, at_r, g1_s, g1_r, g2_s, g2_r, g3_s, g3_r,
):
    T = kv_ref.shape[0]
    D = wall.shape[3]
    NB, NQ = NZ, NY * CORES
    U = NQ // 2
    H = NB // 2
    RW = DH // NQ
    YL = 2 if NMP % 2 == 0 else 1
    X = NMP // YL
    CUTS = ((0, 144), (144, 128))
    SCALE = DH**-0.5

    seq = lax.axis_index("seq")
    mp = lax.axis_index("mp")
    core = seq % CORES
    z = (seq // CORES) % NZ
    y = seq // (CORES * NZ)

    def zdev(o):
        return ((y * NZ + (z + o + NZ) % NZ) * CORES + core, mp)

    def qoff(i):
        return offset_of(i // 2) % NY, i % 2

    def qdev(i):
        dy, dc = qoff(i)
        return ((((y + dy) % NY) * NZ + z) * CORES + (core + dc) % 2, mp)

    def qabs(i):
        dy, dc = qoff(i)
        return ((y + dy) % NY) * CORES + (core + dc) % 2

    def qback(i):
        dy, dc = qoff(i)
        return 2 * place(-dy, NY) + dc

    def mdev(r):
        return (seq, (mp + r) % NMP)

    def head_at(flip, dx):
        return ((mp // X + flip) % YL) * X + (mp % X + dx + X) % X

    partner = qdev(1)

    def rcopy(src, dst, ssem, rsem, dev):
        return pltpu.make_async_remote_copy(
            src_ref=src, dst_ref=dst, send_sem=ssem, recv_sem=rsem, device_id=dev, device_id_type=MESH
        )

    barrier = pltpu.get_barrier_semaphore()
    near = [zdev(offset_of(j)) for j in range(1, min(NB, 3))] + [partner]
    near += [qdev(2 * k) for k in range(1, min(NY, 3))]
    near += [(seq, head_at(1, 0))] * (YL - 1) + [(seq, head_at(0, dx)) for dx in range(1, X)]
    for dev in near:
        pl.semaphore_signal(barrier, inc=1, device_id=dev, device_id_type=MESH)

    w_ref = wall.at[mp]
    loads = [
        pltpu.make_async_copy(a, b, in_sem.at[n])
        for n, (a, b) in enumerate(((kv_hbm, kv_ref), (qT_hbm, qT_ref), (w_hbm, w_ref), (g_hbm, g_ref), (fill_hbm, fill_ref)))
    ]
    for c in loads:
        c.start()

    rows = lax.broadcasted_iota(jnp.int32, (T, 1), 0)
    loads[4].wait()
    fills = [fill_ref[t] for t in range(T // TILE)]
    live_col = jnp.zeros((T, 1), F32)
    for t in range(T // TILE):
        inside = (rows >= t * TILE) & (rows < t * TILE + fills[t])
        live_col = jnp.where(inside, 1.0, live_col)
    lanes = lax.broadcasted_iota(jnp.int32, (1, T), 1)
    live_row = jnp.zeros((1, T), F32)
    for t in range(T // TILE):
        inside = (lanes >= t * TILE) & (lanes < t * TILE + fills[t])
        live_row = jnp.where(inside, 1.0, live_row)
    loads[0].wait()
    kv = kv_ref[...].astype(F32)
    is_key = lax.broadcasted_iota(jnp.int32, (1, 2 * DH), 1) < DH
    stand_in = jnp.where(is_key, kv[0:1, :], 0.0)
    kvb[0, 0:T, :] = jnp.where(live_col > 0.0, kv, stand_in).astype(BF)
    tail_rows = lax.broadcasted_iota(jnp.int32, (16, 1), 0)
    tail = jnp.zeros((16, TILE), F32)
    for t in range(T // TILE):
        tail = jnp.where(tail_rows == t, live_row[:, t * TILE : (t + 1) * TILE], tail)
    kvb[0, T : T + 16, :] = tail.astype(BF)
    loads[1].wait()
    qq[0] = (qT_ref[...].astype(F32) * SCALE).astype(BF)

    def prepare_keys(j):
        live16 = kvb[j, T : T + 16, :].astype(F32)
        row = jnp.concatenate([live16[t : t + 1, :] for t in range(T // TILE)], axis=1)
        kvT[j, 0 : 2 * DH, :] = (kvb[j, 0:T, :].astype(F32).T * row).astype(BF)
        kvT[j, 2 * DH : 2 * DH + 16, :] = jnp.broadcast_to(row, (16, T)).astype(BF)

    def prepare_queries(i):
        qS[i, 0:DH, :] = qq[i]

    pl.semaphore_wait(barrier, len(near))

    copies = []

    def send(src, dst, ssem, rsem, dev):
        rcopy(src, dst, ssem, rsem, dev).start()
        copies.append(lambda: (src, ssem))

    def send_row(buf, a, b, ssem, k, rsem, dev):
        rcopy(buf.at[a], buf.at[b], ssem.at[k], rsem, dev).start()
        copies.append(lambda: (buf.at[(0, 0) if isinstance(a, tuple) else 0], ssem.at[k]))

    def arrive(dst, rsem):
        rcopy(dst, dst, kv0_s.at[0], rsem, partner).wait_recv()

    def send_keys(j, hf, to, sem, k, dev):
        lo, size = CUTS[hf]
        src, dst = kvb.at[j, pl.ds(lo, size)], kvb.at[to, pl.ds(lo, size)]
        rcopy(src, dst, sem.at[k], kv_r.at[2 * to + hf], dev).start()
        copies.append(lambda: (kvb.at[0, pl.ds(lo, size)], sem.at[k]))

    right = place(-1, NZ)
    for hf in range(2):
        if NZ > 2 or hf == 0:
            send_keys(0, hf, right, kv0_s, hf, zdev(1))
        if NZ > 2 or hf == 1:
            send_keys(0, hf, 1, kv0_s, 2 + hf, zdev(-1))

    def spread(buf, ssem, rsem):
        for k in range(1, min(NY, 3)):
            i, back = 2 * k, qback(2 * k)
            send(buf.at[0], buf.at[back], ssem.at[i], rsem.at[back], qdev(i))
        send(buf.at[0], buf.at[1], ssem.at[1], rsem.at[1], partner)

    spread(qq, q_s, q_r)
    loads[2].wait()
    loads[3].wait()
    gmb[...] = (g_ref[...].astype(F32) * live_col).astype(BF)
    dd[0] = nt(wall[mp].reshape(DH, D), gmb[...]).astype(BF)
    spread(dd, d_s, d_r)
    if YL == 2:
        send_row(wall, (mp, core), (mp, core), w_s, 0, w_r.at[0], (seq, head_at(1, 0)))
    prepare_keys(0)
    prepare_queries(0)
    for i in range(NQ):
        qS[i, DH : 2 * DH, :] = jnp.zeros((DH, T), BF)
        wq[i, DH : 2 * DH, :] = jnp.zeros((DH, T), BF)

    for i in range(NQ):
        m[i] = jnp.full((8, T), -1e30, F32)
        oacc[i] = jnp.zeros((2 * DH + 16, T), F32)
        dqacc[i] = jnp.zeros((DH, T), F32)

    def relay(buf, lsem, rsem, k):
        i = 2 * k
        arrive(buf.at[i], rsem.at[i])
        send_row(buf, i, i + 1, lsem, i, rsem.at[i + 1], partner)

    def half_of(k):
        return pl.ds((k - 1) * (DH // 2), DH // 2)

    def send_half(buf, k, ssem, rsem):
        src, dst = buf.at[2 * k, half_of(k)], buf.at[6, half_of(k)]
        rcopy(src, dst, ssem.at[k - 1], rsem.at[k - 1], qdev(6 - 2 * k)).start()
        copies.append(lambda: (buf.at[0, half_of(k)], ssem.at[k - 1]))

    def forward_keys(j, hf):
        arrive(kvb.at[j, pl.ds(*CUTS[hf])], kv_r.at[2 * j + hf])
        k = (j + 1) // 2
        odd = j % 2 == 1
        if j < NZ - 1 and (k + 1 < NZ // 2 or hf == (1 if odd else 0)):
            to = j + 2 if k + 1 < NZ // 2 else NZ - 1
            send_keys(j, hf, to, kv_s, 2 * j + hf, zdev(-1 if odd else 1))

    def before(it):
        def take(js):
            for hf in range(2):
                for j in js:
                    forward_keys(j, hf)

        js = []
        if it == 0 and H > 1:
            js = [1, 2]
        if it > 1 and it + 1 < H:
            js = [2 * it + 1, 2 * it + 2]
        if it == NB - 1:
            js = [NB - 1]
        take(js)
        if it == 0:
            for k in range(1, min(NY, 3)):
                relay(qq, ql_s, q_r, k)
                if NY == 4:
                    send_half(qq, k, qf_s, qf_r)
            if H > 2:
                take([3, 4])
                js = js + [3, 4]
        if it == min(1, H // 2) and NY == 4:
            for k in range(1, 3):
                arrive(qq.at[6, half_of(k)], qf_r.at[k - 1])
            send_row(qq, 6, 7, ql_s, 6, q_r.at[7], partner)
        for half in range(2):
            if it == half * (H // 2):
                for i in range(half * U, half * U + U):
                    if i % 2 == 1:
                        arrive(qq.at[i], q_r.at[i])
                    if i > 0:
                        prepare_queries(i)
        for j in js:
            prepare_keys(j)
        if it == max(NB - 5, 0):
            if YL == 2:
                arrive(wall.at[0, 0], w_r.at[0])
            for dx in range(1, X):
                for flip in range(YL):
                    k = 1 + 2 * (dx - 1) + flip
                    h = head_at(flip, 0)
                    send_row(wall, (h, core), (h, core), w_s, k, w_r.at[k], (seq, head_at(0, dx)))
        if it == 1:
            for k in range(1, min(NY, 3)):
                relay(dd, dl_s, d_r, k)
                if NY == 4:
                    send_half(dd, k, df_s, df_r)
        if it == max(NB - 2, 1) and NY == 4:
            for k in range(1, 3):
                arrive(dd.at[6, half_of(k)], df_r.at[k - 1])
            send_row(dd, 6, 7, dl_s, 6, d_r.at[7], partner)

    def step_of(n):
        late = n - 2 * H
        if isinstance(n, int):
            j = n if n < H else (n - H if late < 0 else H + late // 2)
            return j, U * (0 if n < H else (1 if late < 0 else late % 2))
        j = jnp.where(n < H, n, jnp.where(late < 0, n - H, H + jnp.right_shift(late, 1)))
        half = jnp.where(n < H, 0, jnp.where(late < 0, 1, late & 1))
        return j, half * U

    def S(n, buf):
        j, i0 = step_of(n)
        for t in range(U):
            buf[t] = nn(kvb[j, 0:T, :], qS[i0 + t])

    def E(n, buf, par):
        j, i0 = step_of(n)
        for t in range(U):
            i = i0 + t
            m_old = m[i, 0:1, :]
            m_new = jnp.maximum(m_old, jnp.max(buf[t], axis=0, keepdims=True))
            mh[j, i, 0:1, :] = m_new
            m[i, 0:1, :] = m_new
            ab[par, t, 0:1, :] = jnp.exp(m_old - m_new)
            p[j, i] = jnp.exp(buf[t] - m_new).astype(BF)

    def O(n, par):
        j, i0 = step_of(n)
        for t in range(U):
            i = i0 + t
            oacc[i] = oacc[i] * ab[par, t, 0:1, :] + nn(kvT[j], p[j, i])

    before(0)
    first, last = 0, 2 * NB - 1
    S(first, sA)
    E(first, sA, 0)
    S(first + 1, sB)

    @pl.loop(1, NB)
    def _(it):
        for fixed in range(1, NB):
            if fixed in WAITS(NB, H):
                pl.when(it == fixed)(functools.partial(before, fixed))
        n = 2 * it
        S(n, sA)
        E(n - 1, sB, 1)
        O(n - 2, 0)
        S(n + 1, sB)
        E(n, sA, 0)
        O(n - 1, 1)

    E(last, sB, 1)
    O(last - 1, 0)
    O(last, 1)
    for k in range(NY):
        arrive(dd.at[2 * k + 1], d_r.at[2 * k + 1])

    for i in range(NQ):
        total = oacc[i, 2 * DH : 2 * DH + 1, :]
        inv = 1.0 / total
        o = oacc[i, DH : 2 * DH, :] * inv
        oacc[i, 0:DH, :] = oacc[i, 0:DH, :] * inv
        osend[i % 2, i // 2] = o.astype(BF)
        lrow = m[i, 0:1, :] + jnp.log(total)
        drow = jnp.sum(o * dd[i].astype(F32), axis=0, keepdims=True)
        Ll[i, 0:1, :] = lrow
        Dl[i, 0:1, :] = drow
        stl[pl.ds(qabs(i), 1), :] = lrow
        stl[pl.ds(NQ + qabs(i), 1), :] = drow

    send(stl, pst, st_s.at[NY], st_r.at[NY], partner)
    for k in reversed(range(NY)):
        send(osend.at[1, k], opair.at[k], o_s.at[NY + k], o_r.at[NY + k], partner)

    def chip_totals():
        arrive(pst, st_r.at[NY])
        la, lb = stl[0:NQ, :], pst[0:NQ, :]
        top = jnp.maximum(la, lb)
        wa, wb = jnp.exp(la - top), jnp.exp(lb - top)
        both = wa + wb
        inv = 1.0 / both
        str_[0, 0:NQ, :] = top + jnp.log(both)
        str_[0, NQ : 2 * NQ, :] = (wa * stl[NQ : 2 * NQ, :] + wb * pst[NQ : 2 * NQ, :]) * inv
        for k in range(1, NY):
            back = qback(2 * k) // 2
            send(str_.at[0], str_.at[back], st_s.at[k], st_r.at[back], qdev(2 * k))
        wpair[0] = wa * inv
        wpair[1] = wb * inv
        for k in reversed(range(NY)):
            arrive(opair.at[k], o_r.at[NY + k])
            row = pl.ds(qabs(2 * k), 1)
            mine = osend[0, k].astype(F32) * wpair[0, row, :]
            osend[0, k] = (mine + opair[k].astype(F32) * wpair[1, row, :]).astype(BF)
            if k > 0:
                back = qback(2 * k) // 2
                send(osend.at[0, k], orecv.at[back], o_s.at[k], o_r.at[back], qdev(2 * k))

    def Ust(j, half, buf):
        for t in range(U):
            i = half * U + t
            c = jnp.exp(mh[j, i, 0:1, :] - Ll[i, 0:1, :])
            rhs = jnp.concatenate([jnp.zeros((DH, T), BF), (dd[i].astype(F32) * c).astype(BF)], axis=0)
            buf[t] = nn(kvb[j, 0:T, :], rhs) - c * Dl[i, 0:1, :]

    def Dst(j, half, buf):
        for t in range(U):
            i = half * U + t
            ds[j, i] = p[j, i] * buf[t].astype(BF)

    def Mst(j, half):
        for t in range(U):
            i = half * U + t
            dqacc[i] += nn(kvT[j, 0:DH, :], ds[j, i])

    Ust(0, 0, sA)
    Dst(0, 0, sA)
    Ust(0, 1, sB)

    def local_turn(j):
        Ust(j, 0, sA)
        Dst(j - 1, 1, sB)
        Mst(j - 1, 0)
        Ust(j, 1, sB)
        Dst(j, 0, sA)
        Mst(j - 1, 1)

    cut = min(NB, 2)
    pl.loop(1, cut)(local_turn)
    chip_totals()
    pl.loop(cut, NB)(local_turn)
    Dst(NB - 1, 1, sB)
    Mst(NB - 1, 0)
    Mst(NB - 1, 1)

    for k in range(1, NY):
        arrive(str_.at[k], st_r.at[k])
    big = str_[0, 0:NQ, :]
    for k in range(1, NY):
        big = jnp.maximum(big, str_[k, 0:NQ, :])
    wsum = jnp.zeros((NQ, T), F32)
    dsum = jnp.zeros((NQ, T), F32)
    for k in range(NY):
        wt = jnp.exp(str_[k, 0:NQ, :] - big)
        wsum = wsum + wt
        dsum = dsum + wt * str_[k, NQ : 2 * NQ, :]
    Lg[0:NQ, :] = big + jnp.log(wsum)
    Dg[0:NQ, :] = dsum / wsum
    def attended_rows():
        own = pl.ds(qabs(0), 1)
        att = jnp.exp(str_[0, own, :] - Lg[own, :]) * osend[0, 0].astype(F32)
        for k in range(1, NY):
            arrive(orecv.at[k], o_r.at[k])
            att = att + jnp.exp(str_[k, own, :] - Lg[own, :]) * orecv[k].astype(F32)
        wgp = nn(att.astype(BF), gmb[...])
        for s in range(NQ):
            wg1s[s] = wgp[s * RW : (s + 1) * RW, :].astype(BF)
        for i in range(1, NQ):
            back = qback(i)
            send(wg1s.at[qabs(i)], wg1r.at[back], g1_s.at[i], g1_r.at[back], qdev(i))
        attall[mp] = (att * live_row).astype(BF)
        for dx in range(1, X):
            for flip in range(YL):
                arrive(wall.at[0, 0], w_r.at[1 + 2 * (dx - 1) + flip])
        for r in range(1, NMP):
            send(attall.at[mp], attall.at[mp], at_s.at[r], at_r.at[r], mdev(r))

    for i in range(NQ):
        w = jnp.exp(Ll[i, 0:1, :] - Lg[pl.ds(qabs(i), 1), :])
        e = w * (Dl[i, 0:1, :] - Dg[pl.ds(qabs(i), 1), :])
        q32 = qq[i].astype(F32)
        wq[i, 0:DH, :] = (q32 * w).astype(BF)
        rr[i, 0:DH, :] = q32 * e
        rr[i, DH : 2 * DH, :] = dd[i].astype(F32) * w
        total = (dqacc[i] * w + oacc[i, 0:DH, :] * e) * SCALE
        if i == 0:
            dqacc[0] = total
        else:
            dqacc[i] = total
            if i % 2 == 1:
                dqsend[1, i // 2] = total.astype(BF)

    def key_pair(n):
        @pl.loop(0, 2)
        def _(b):
            j = NB - 1 - 2 * n - b
            acc = None
            for i in range(NQ):
                c = jnp.exp(mh[j, i, 0:1, :] - Ll[i, 0:1, :])
                r = nt(ds[j, i], wq[i]) + nt(p[j, i], (rr[i] * c).astype(BF))
                acc = r if acc is None else acc + r
            dkp[j] = acc

    def pass_on(j, hf):
        lo, size = hf * (T // 2), T // 2
        total = dkp[j, pl.ds(lo, size), :]
        odd = j % 2 == 1
        if j < NZ - 3 or (j == NZ - 3 and hf == 0) or (j == NZ - 2 and hf == 1):
            arrive(drecv.at[j, pl.ds(lo, size)], dk_r.at[2 * j + hf])
            total = total + drecv[j, pl.ds(lo, size), :].astype(F32)
        dsend[j, pl.ds(lo, size), :] = total.astype(BF)
        if j == NZ - 1:
            onward = hf == 0
            to = max(NZ - 3, 0) if hf == 0 else max(NZ - 2, 1)
        else:
            onward = odd
            to = j - 2 if j >= 3 else (0 if j == 1 else NZ - 1)
        send(dsend.at[j, pl.ds(lo, size)], drecv.at[to, pl.ds(lo, size)], dk_s.at[2 * j + hf], dk_r.at[2 * to + hf],
             zdev(1 if onward else -1))

    def gradient_over_z():
        wg1r[0] = wg1s[qabs(0)]
        for i in range(1, NQ):
            arrive(wg1r.at[i], g1_r.at[i])
        part = wg1r[0].astype(F32)
        for i in range(1, NQ):
            part = part + wg1r[i].astype(F32)
        wg2[z] = part.astype(BF)
        for r in range(1, NZ):
            send(wg2.at[z], wg2.at[z], g2_s.at[r], g2_r.at[r], zdev(r))

    def less_urgent():
        arrive(dqpair, dq_r.at[NY])
        dqacc[0] += dqpair[0].astype(F32)
        for k in range(1, NY):
            dqsend[0, k] = (dqacc[2 * k] + dqpair[k].astype(F32)).astype(BF)
            back = qback(2 * k) // 2
            send(dqsend.at[0, k], dqrecv.at[back], dq_s.at[k], dq_r.at[back], qdev(2 * k))
        if YL == 2:
            send_row(wall, (head_at(1, 0), core), (head_at(1, 0), core), wl_s, 0, wl_r.at[0], partner)
        for dx in range(1, X):
            for flip in range(YL):
                k = 1 + 2 * (dx - 1) + flip
                h = head_at(flip, -dx)
                send_row(wall, (h, core), (h, core), wl_s, k, wl_r.at[k], partner)

    for n in range(H):
        key_pair(n)
        if n == H - 2 and n > 0:
            gradient_over_z()
        j = NB - 1 - 2 * n
        pass_on(j, 0)
        if n > 0:
            pass_on(j + 1, 1)
        pass_on(j, 1)
        if j > 1:
            pass_on(j - 1, 0)
        if n == 0:
            attended_rows()
            send(dqsend.at[1], dqpair, dq_s.at[NY], dq_r.at[NY], partner)
        if n == min(1, H - 1):
            less_urgent()
    if H <= 2:
        gradient_over_z()

    for r in range(1, NZ):
        arrive(wg2.at[0], g2_r.at[r])
    part = wg2[0].astype(F32)
    for k in range(1, NZ):
        part = part + wg2[k].astype(F32)
    own = qabs(0)
    wg3[own] = part.astype(BF)
    for i in range(1, NQ):
        send(wg3.at[own], wg3.at[own], g3_s.at[i], g3_r.at[qback(i)], qdev(i))

    for r in range(1, NMP):
        arrive(wall.at[0, 0], wl_r.at[r - 1])
        arrive(attall.at[0], at_r.at[r])
    att_rows = attall[...].reshape(NMP * DH, T).astype(F32).T.astype(BF)
    out_ref[...] = nn(att_rows, wall[...].reshape(NMP * DH, D)).astype(BF)

    total = dqacc[0]
    for k in range(1, NY):
        arrive(dqrecv.at[k], dq_r.at[k])
        total = total + dqrecv[k].astype(F32)
    dq_ref[...] = total

    for hf in range(2):
        rows_of = pl.ds(hf * (T // 2), T // 2)
        total = dkp[0, rows_of, :]
        for slot in (0, NB - 1):
            if NZ > 2 or slot == hf:
                arrive(drecv.at[slot, rows_of], dk_r.at[2 * slot + hf])
                total = total + drecv[slot, rows_of, :].astype(F32)
        dkv_ref[rows_of, :] = total * live_col[hf * (T // 2) : (hf + 1) * (T // 2), :]

    for i in range(1, NQ):
        arrive(wg3.at[0], g3_r.at[i])
    for s in range(NQ):
        wg_ref[s * RW : (s + 1) * RW, :] = wg3[s].astype(F32)

    for make in copies:
        src, ssem = make()
        rcopy(src, src, ssem, kv_r.at[0], partner).wait_send()


def WAITS(NB, H):
    return set(range(1, H - 1)) | {1} | {H // 2, NB - 1, max(NB - 5, 0), max(NB - 2, 0)}


def write_out(a_ref, b_ref, c_ref, d_ref, a_hbm, b_hbm, c_hbm, d_hbm, sem):
    pairs = ((a_ref, a_hbm), (b_ref, b_hbm), (c_ref, c_hbm), (d_ref, d_hbm))
    copies = [pltpu.make_async_copy(r, h, sem.at[n]) for n, (r, h) in enumerate(pairs)]
    for c in copies:
        c.start()
    for c in copies:
        c.wait()


def solution(mesh):
    NMP = mesh.shape["mp"]
    NSEQ = mesh.shape["seq"]
    NY, NZ = {64: (4, 8), 8: (2, 2), 16: (2, 4)}[NSEQ]
    NB, NQ = NZ, NY * CORES
    U = NQ // 2

    def shards(queries, key_value, tile_fill, out_weight, grad_output):
        T = queries.shape[0]
        D = out_weight.shape[2]
        qT = queries[:, 0, :].T
        kv = key_value[:, 0, :]
        w = out_weight.reshape(CORES, DH // CORES, out_weight.shape[2])
        V = pl.BlockSpec(memory_space=pltpu.VMEM)
        A = pl.BlockSpec(memory_space=pl.ANY)
        v = pltpu.VMEM
        dma = lambda n: pltpu.SemaphoreType.DMA((n,))
        RW = DH // NQ
        scratch = [
            pltpu.SMEM((T // TILE,), jnp.int32), v((DH, T), BF), v((T, 2 * DH), BF), v((T, D), BF), dma(5),
            v((NB, T + 16, 2 * DH), BF), v((NB, 2 * DH + 16, T), BF), v((NQ, DH, T), BF), v((NQ, DH, T), BF),
            v((NQ, 2 * DH, T), BF), v((NB, NQ, T, T), BF), v((NB, NQ, 8, T), F32), v((NQ, 8, T), F32),
            v((NQ, 2 * DH + 16, T), F32), v((2, U, 8, T), F32), v((NB, NQ, T, T), BF),
            v((U, T, T), F32), v((U, T, T), F32), v((NQ, 8, T), F32), v((NQ, 8, T), F32),
            v((NQ, 2 * DH, T), F32), v((NQ, 2 * DH, T), BF),
            v((2 * NQ, T), F32), v((2 * NQ, T), F32), v((NY, 2 * NQ, T), F32), v((2, NQ, T), F32), v((8, T), F32), v((8, T), F32),
            v((2, NY, DH, T), BF), v((NY, DH, T), BF), v((NY, DH, T), BF), v((NB, T, 2 * DH), F32), v((NB, T, 2 * DH), BF), v((NB, T, 2 * DH), BF),
            v((NQ, DH, T), F32), v((2, NY, DH, T), BF), v((NY, DH, T), BF), v((NY, DH, T), BF),
            v((T, D), BF), v((NMP, CORES, DH // CORES, D), BF), v((NMP, DH, T), BF),
            v((NQ, RW, D), BF), v((NQ, RW, D), BF), v((NZ, RW, D), BF), v((NQ, RW, D), BF),
            dma(4), dma(2 * NB), dma(2 * NB), dma(2), dma(2), dma(2), dma(2), dma(NQ), dma(NQ), dma(NQ), dma(NQ), dma(NQ), dma(NQ), dma(NQ), dma(NQ),
            dma(NQ), dma(NQ), dma(2 * NB), dma(2 * NB), dma(NQ), dma(NQ),
            dma(NMP), dma(NMP), dma(NMP), dma(NMP), dma(NMP), dma(NMP), dma(NQ), dma(NQ), dma(NZ), dma(NZ), dma(NQ), dma(NQ),
        ]
        shapes = [((T, D), BF), ((DH, T), F32), ((T, 2 * DH), F32), ((DH, D), F32)]
        results = pl.pallas_call(
            functools.partial(kernel, NY, NZ, NMP),
            name="voxel_attention",
            out_shape=[pltpu.VMEM(*s) for s in shapes],
            in_specs=[A, A, A, A, A],
            out_specs=[V, V, V, V],
            scratch_shapes=scratch,
            compiler_params=pltpu.CompilerParams(
                collective_id=0, has_side_effects=True, vmem_limit_bytes=56 * 1024 * 1024
            ),
        )(tile_fill, qT, kv, w, grad_output)
        out, dqT, dkv, wg = pl.pallas_call(
            write_out,
            name="write_out",
            out_shape=[jax.ShapeDtypeStruct(*s) for s in shapes],
            in_specs=[V, V, V, V],
            out_specs=[A, A, A, A],
            scratch_shapes=[dma(4)],
        )(*(pltpu.with_memory_space_constraint(r, pltpu.VMEM) for r in results))
        return out, dqT.T[:, None, :], dkv[:, None, :], wg[None]

    return jax.shard_map(
        shards,
        mesh=mesh,
        in_specs=(
            P("seq", "mp", None),
            P("seq", "mp", None),
            P("seq"),
            P("mp", None, None),
            P("seq", None),
        ),
        out_specs=(P("seq", None), P("seq", "mp", None), P("seq", "mp", None), P("mp", None, None)),
        check_vma=False,
    )
```
